32 devices in a mesh: dp: 4 (over y, x), row: 2 (over core), col: 4 (over z).
Axes of the slice: x: 2, y: 2, z: 4, core: 2. Of those that a mesh axis runs over, the one named last changes fastest.
Arguments:
- tokens: float32 [32768, 768], P(('dp', 'row', 'col')), may hold values from -6 to 6
- segments: int32 [32768], P(('dp', 'row', 'col')), may hold values from 0 to 17, as said below
- cotangent: float32 [32768, 768], P(('dp', 'row', 'col')), may hold values from -6 to 6
- qkv_weight: bfloat16 [768, 2304], P('row', 'col'), may hold values from -0.21875 to 0.21875
- out_weight: bfloat16 [768, 768], P('row', 'col'), may hold values from -0.875 to 0.875
- up_weight: bfloat16 [768, 3072], P('row', 'col'), may hold values from -0.21875 to 0.21875
- down_weight: bfloat16 [3072, 768], P('row', 'col'), may hold values from -0.109375 to 0.109375
- qv_bias: bfloat16 [1536], P(('row', 'col')), may hold values from -3 to 3
- out_bias: bfloat16 [768], P(('row', 'col')), may hold values from -2 to 2
- norm1_gain: bfloat16 [768], P(('row', 'col')), may hold values from 0.25 to 1.75
- norm1_shift: bfloat16 [768], P(('row', 'col')), may hold values from -2 to 2
- up_bias: bfloat16 [3072], P(('row', 'col')), may hold values from -3 to 3
- down_bias: bfloat16 [768], P(('row', 'col')), may hold values from -2 to 2
- norm2_gain: bfloat16 [768], P(('row', 'col')), may hold values from 0.25 to 1.75
- norm2_shift: bfloat16 [768], P(('row', 'col')), may hold values from -2 to 2
Outputs:
- layer_out: float32 [32768, 768], P(('dp', 'row', 'col'))
- token_grad: float32 [32768, 768], P(('dp', 'row', 'col'))
- qkv_weight_grad: float32 [768, 2304], P('row', 'col')
- out_weight_grad: float32 [768, 768], P('row', 'col')
- up_weight_grad: float32 [768, 3072], P('row', 'col')
- down_weight_grad: float32 [3072, 768], P('row', 'col')
- qv_bias_grad: float32 [1536], P(('row', 'col'))
- out_bias_grad: float32 [768], P(('row', 'col'))
- norm1_gain_grad: float32 [768], P(('row', 'col'))
- norm1_shift_grad: float32 [768], P(('row', 'col'))
- up_bias_grad: float32 [3072], P(('row', 'col'))
- down_bias_grad: float32 [768], P(('row', 'col'))
- norm2_gain_grad: float32 [768], P(('row', 'col'))
- norm2_shift_grad: float32 [768], P(('row', 'col'))
The draws below stay inside these ranges and needn't reach their ends.
Inputs may be any that keep to these rules, and one draw needn't show every extreme that they name: `segments`: in each sequence of 1024 consecutive tokens, whole documents of 60 to 800 tokens are numbered 1, 2, 3, ... in order from the sequence's start, and the remaining tail (fewer than 800 tokens, possibly none) is 0. The first sequence of the batch holds documents of exactly 60 tokens.
All inputs are finite; a program needn't handle non-finite values.
Results may differ from the reference program's by a relative error of at most 0.015.
Values may be sent and summed in bfloat16 or wider, within the bound.
No kernel may reach another device: no remote copies, remote signals or barrier semaphores. Data moves between devices by JAX's collectives and lax.ppermute only.
A program may use at most 256 MiB of HBM per device.

```python
import math
import jax
import jax.numpy as jnp
from jax import lax

D = 768
HEADS = 12
FF = 3072
SEQ = 1024
DOC_MIN = 60
DOC_MAX = 800
TOKENS = 32768


def draw_segments(key, part):
    seq_count = TOKENS // SEQ
    slots = SEQ // DOC_MIN + 1
    lengths = jax.random.randint(key, (seq_count, slots), DOC_MIN, DOC_MAX + 1)
    first_seq = jnp.arange(seq_count)[:, None] == 0
    lengths = jnp.where(first_seq, DOC_MIN, lengths).astype(jnp.int32)
    ends = jnp.cumsum(lengths, axis=1)
    places = jnp.arange(SEQ, dtype=jnp.int32)
    index = jnp.sum((ends[:, None, :] <= places[None, :, None]).astype(jnp.int32), axis=2)
    end_here = jnp.take_along_axis(ends, index, axis=1)
    labels = jnp.where(end_here <= SEQ, index + 1, 0)
    return labels.reshape(-1).astype(jnp.int32)


def block_scale(own_key, dims, pieces, smallest, largest):
    def one(dim, blocks):
        draws = jax.random.uniform(jax.random.fold_in(jax.random.fold_in(own_key, 6), dim), (blocks,), jnp.float32, smallest / len(pieces), largest / len(pieces))
        return jnp.repeat(jnp.exp(draws), dims[dim] // blocks).reshape((-1,) + (1,) * (len(dims) - dim - 1))

    loudness = one(*pieces[0])
    for cut in pieces[1:]:
        loudness = loudness * one(*cut)
    return loudness


def centred(stream_key, extent, deviation, most, cuts=(), kind=jnp.bfloat16):
    entries = jax.random.normal(stream_key, extent, jnp.float32) * deviation
    if len(cuts) > 0:
        entries = block_scale(stream_key, extent, cuts, -0.22, 0.18) * entries
    return jnp.clip(entries, min=-most, max=most).astype(kind)


def setup_inputs(seed: int = 0) -> dict:
    keys = jax.random.split(jax.random.key(seed), 16)
    tokens = centred(keys[0], (TOKENS, D), 1.0, 6.0, ((0, 32),), jnp.float32)
    segments = draw_segments(jax.random.fold_in(keys[15], 71), 0)
    cotangent = centred(keys[2], (TOKENS, D), 1.0, 6.0, ((0, 32),), jnp.float32)
    qkv_weight = centred(keys[3], (D, 3 * D), D ** -0.5, 0.21875, ((0, 2), (1, 4)))
    out_weight = centred(keys[4], (D, D), (D // 16) ** -0.5, 0.875, ((0, 2), (1, 4)))
    up_weight = centred(keys[5], (D, FF), D ** -0.5, 0.21875, ((0, 2), (1, 4)))
    down_weight = centred(keys[6], (FF, D), FF ** -0.5, 0.109375, ((0, 2), (1, 4)))
    qv_bias = centred(keys[7], (2 * D,), 0.5, 3.0, ((0, 8),))
    out_bias = centred(keys[8], (D,), 0.3, 2.0, ((0, 8),))
    norm1_gain = jnp.clip(1.0 + 0.15 * jax.random.normal(keys[9], (D,), jnp.float32), 0.25, 1.75).astype(jnp.bfloat16)
    norm1_shift = centred(keys[10], (D,), 0.3, 2.0, ((0, 8),))
    up_bias = centred(keys[11], (FF,), 0.5, 3.0, ((0, 8),))
    down_bias = centred(keys[12], (D,), 0.3, 2.0, ((0, 8),))
    norm2_gain = jnp.clip(1.0 + 0.15 * jax.random.normal(keys[13], (D,), jnp.float32), 0.25, 1.75).astype(jnp.bfloat16)
    norm2_shift = centred(keys[14], (D,), 0.3, 2.0, ((0, 8),))
    return {"tokens": tokens, "segments": segments, "cotangent": cotangent, "qkv_weight": qkv_weight, "out_weight": out_weight, "up_weight": up_weight, "down_weight": down_weight, "qv_bias": qv_bias, "out_bias": out_bias, "norm1_gain": norm1_gain, "norm1_shift": norm1_shift, "up_bias": up_bias, "down_bias": down_bias, "norm2_gain": norm2_gain, "norm2_shift": norm2_shift}


@jax.custom_vjp
def low(v):
    return lax.optimization_barrier(v.astype(jnp.bfloat16)).astype(jnp.float32)

@jax.custom_vjp
def low_back(v):
    return v

def low_keep(v):
    return (low(v), None)

def low_pass(kept, grad):
    return (grad,)

def back_keep(v):
    return (v, None)

def back_low(kept, grad):
    return (low(grad),)
low.defvjp(low_keep, low_pass)
low_back.defvjp(back_keep, back_low)
EPS = 1e-05
NEG = -1e+30
HIGHEST = lax.Precision.HIGHEST

def layer_norm(hidden, gain, shift):
    center = hidden - lax.optimization_barrier(jnp.mean(hidden, axis=-1, keepdims=True))
    spread = lax.optimization_barrier(jnp.mean(center * center, axis=-1, keepdims=True))
    return center * lax.rsqrt(spread + EPS) * gain + shift

def product(left, right):
    return jnp.dot(left, right, precision=HIGHEST)

def attend_group(group_in):
    queries, keys_in, values_in, seg_in = group_in
    scaling = queries.shape[-1] ** (-0.5)
    scores = low_back(jnp.einsum('gqhd,gkhd->ghqk', queries, keys_in, precision=HIGHEST) * scaling)
    places = jnp.arange(queries.shape[1])
    same_doc = (seg_in[:, :, None] == seg_in[:, None, :]) & (seg_in[:, None, :] != 0)
    allowed = same_doc | (places[:, None] == places[None, :])[None]
    scores = jnp.where(allowed[:, None], scores, NEG)
    row_peak = lax.optimization_barrier(jnp.max(scores, axis=-1, keepdims=True))
    exp_scores = jnp.exp(scores - row_peak)
    probs = exp_scores / lax.optimization_barrier(jnp.sum(exp_scores, axis=-1, keepdims=True))
    return jnp.einsum('ghqk,gkhd->gqhd', low(probs), values_in, precision=HIGHEST)

def forward(inputs, params, segments):
    qkv_weight, out_weight, up_weight, down_weight, qv_bias, out_bias, norm1_gain, norm1_shift, up_bias, down_bias, norm2_gain, norm2_shift = params
    count, width = inputs.shape
    head_dim = width // HEADS
    seq_count = count // SEQ
    group_n = math.gcd(seq_count, max(1, 4096 // SEQ))
    mixed = product(low(inputs), qkv_weight)
    queries = low(low_back(mixed[:, :width] + qv_bias[:width]))
    keys_all = low(low_back(mixed[:, width:2 * width]))
    values_all = low(low_back(mixed[:, 2 * width:] + qv_bias[width:]))

    def grouped(array):
        return array.reshape(seq_count // group_n, group_n, SEQ, HEADS, head_dim)
    attended = lax.map(jax.checkpoint(attend_group), (grouped(queries), grouped(keys_all), grouped(values_all), segments.reshape(seq_count // group_n, group_n, SEQ)))
    attended = low(low_back(attended.reshape(count, width)))
    branch = low_back(product(attended, out_weight) + out_bias)
    normed = layer_norm(inputs + branch, norm1_gain, norm1_shift)
    pre_act = low_back(product(low(normed), up_weight) + up_bias)
    activated = low(jax.nn.gelu(pre_act, approximate=False))
    feed_out = low_back(product(activated, down_weight) + down_bias)
    return layer_norm(normed + feed_out, norm2_gain, norm2_shift)

def reference(tokens, segments, cotangent, qkv_weight, out_weight, up_weight, down_weight, qv_bias, out_bias, norm1_gain, norm1_shift, up_bias, down_bias, norm2_gain, norm2_shift):
    params = tuple((weight_arr.astype(jnp.float32) for weight_arr in (qkv_weight, out_weight, up_weight, down_weight, qv_bias, out_bias, norm1_gain, norm1_shift, up_bias, down_bias, norm2_gain, norm2_shift)))
    live_rows = (segments != 0).astype(jnp.float32)[:, None]
    layer_out, pull = jax.vjp(lambda inputs, weights: forward(inputs, weights, segments), tokens, params)
    token_grad, grads = pull(cotangent * live_rows)
    return (layer_out, token_grad, grads[0], grads[1], grads[2], grads[3], grads[4], grads[5], grads[6], grads[7], grads[8], grads[9], grads[10], grads[11])
```

```python
from functools import partial

import jax
import jax.numpy as jnp
from jax import lax
from jax.experimental import pallas as pl
from jax.experimental.pallas import tpu as pltpu
from jax.sharding import PartitionSpec as P

HEADS = 12
SEQ = 1024
EPS = 1e-05
NEG = -1e30
FLOOR = -1e29

F32 = jnp.float32
BF16 = jnp.bfloat16


def layer_norm(hidden, gain, shift):
    center = hidden - jnp.mean(hidden, axis=-1, keepdims=True)
    spread = jnp.mean(center * center, axis=-1, keepdims=True)
    return center * lax.rsqrt(spread + EPS) * gain + shift


def mat(left, right, dims, kind=F32):
    return lax.dot_general(left, right, ((dims[:1], dims[1:]), ((), ())), preferred_element_type=kind)


def swap(value, axis, step):
    count = lax.axis_size(axis)
    return lax.ppermute(value, axis, [(i, i ^ step) for i in range(count)])


def steps_up(axis):
    count, out, step = lax.axis_size(axis), [], 1
    while step < count:
        out.append(step)
        step *= 2
    return out


def bit_of(axis, step):
    return (lax.axis_index(axis) // step) % 2


def widen(value, axis, step, at):
    other = swap(value, axis, step)
    mine_low = bit_of(axis, step) == 0
    return jnp.where(mine_low, jnp.stack([value, other], at), jnp.stack([other, value], at))


def gather_up(value, axis):
    value = value[None]
    for step in steps_up(axis):
        value = widen(value, axis, step, 0)
        value = value.reshape((-1,) + value.shape[2:])
    return value


def gather_down(value, axis):
    value = value[None]
    for step in steps_up(axis)[::-1]:
        value = widen(value, axis, step, 1)
        value = value.reshape((-1,) + value.shape[2:])
    return value


def halve(value, axis, step, at):
    bit = bit_of(axis, step)
    keep = lax.dynamic_index_in_dim(value, bit, at, keepdims=False)
    send = lax.dynamic_index_in_dim(value, 1 - bit, at, keepdims=False)
    got = swap(send, axis, step)
    return (keep.astype(F32) + got.astype(F32)).astype(value.dtype)


def scatter_up(value, axis):
    for step in steps_up(axis):
        value = value.reshape((value.shape[0] // 2, 2) + value.shape[1:])
        value = halve(value, axis, step, 1)
    return value[0]


def scatter_down(value, axis):
    for step in steps_up(axis)[::-1]:
        value = value.reshape((2, value.shape[0] // 2) + value.shape[1:])
        value = halve(value, axis, step, 0)
    return value[0]


def fetch_weight(block):
    rows, cols = block.shape
    dp_n = lax.axis_size("dp")
    part = rows // (2 * dp_n)
    own = lax.dynamic_index_in_dim(
        block.reshape(2, dp_n, part, cols), lax.axis_index("dp"), 1, keepdims=False
    )
    wide = gather_down(own, "col")
    wide = jnp.transpose(wide, (1, 2, 0, 3)).reshape(2, part, -1)
    first = gather_down(wide[0], "dp")
    second = gather_up(wide[1], "dp")
    half = jnp.stack([first, second]).reshape(rows, -1)
    whole = gather_up(half, "row")
    return whole.reshape(-1, whole.shape[-1])


def spread_grad(grad):
    row_n, col_n, dp_n = lax.axis_size("row"), lax.axis_size("col"), lax.axis_size("dp")
    rows, cols = grad.shape[0] // row_n, grad.shape[1] // col_n
    part = rows // (2 * dp_n)
    half = scatter_down(grad.reshape(row_n, rows, -1), "row")
    half = half.reshape(2, dp_n, part, -1)
    first = scatter_up(half[0], "dp")
    second = scatter_down(half[1], "dp")
    pair = jnp.stack([first, second]).reshape(2, part, col_n, cols)
    pair = scatter_up(jnp.transpose(pair, (2, 0, 1, 3)), "col")
    first = gather_down(pair[0], "dp")
    second = gather_up(pair[1], "dp")
    return jnp.stack([first, second]).reshape(rows, cols).astype(F32)


def fetch_vectors(parts):
    sizes = [p.shape[0] for p in parts]
    flat = gather_up(gather_down(jnp.concatenate(parts), "col"), "row")
    flat = flat.reshape(-1, flat.shape[-1])
    out, at = [], 0
    for size in sizes:
        out.append(flat[:, at : at + size].reshape(-1).astype(F32))
        at += size
    return out


def spread_vectors(parts):
    row_n, col_n = lax.axis_size("row"), lax.axis_size("col")
    blocks = row_n * col_n
    flat = jnp.concatenate([p.reshape(blocks, -1) for p in parts], axis=1)
    flat = flat.reshape(row_n, col_n, -1)
    flat = scatter_down(flat, "row")
    flat = scatter_up(flat, "col")
    for step in steps_up("dp"):
        flat = flat + swap(flat, "dp", step)
    out, at = [], 0
    for p in parts:
        size = p.shape[0] // blocks
        out.append(flat[at : at + size])
        at += size
    return out


CHUNK = 256


def attend_kernel(q_ref, k_ref, v_ref, a_ref, b_ref, o_ref, e_ref, inv_ref, *, dim):
    length = q_ref.shape[0]
    low_lane = lax.broadcasted_iota(jnp.int32, (length, 2 * dim), 1) < dim
    low_row = lax.broadcasted_iota(jnp.int32, (2 * dim, length), 0) < dim
    queries = q_ref[...].astype(F32) * (dim**-0.5)
    keys = k_ref[...].astype(F32)
    marks_q = a_ref[...].astype(F32)
    marks_k = b_ref[...].astype(F32)
    values_t = jnp.transpose(v_ref[...].astype(F32))
    inv_ref[...] = jnp.zeros(inv_ref.shape, F32)
    halves = []
    for head in range(2):
        lanes = low_lane if head == 0 else ~low_lane
        rows = low_row if head == 0 else ~low_row
        q_ext = jnp.where(lanes, queries, marks_q).astype(BF16)
        k_ext = jnp.where(lanes, keys, marks_k).astype(BF16)
        v_ext = jnp.where(rows, values_t, 1.0).astype(BF16)
        pieces = []
        for at in range(0, length, CHUNK):
            scores = mat(k_ext, q_ext[at : at + CHUNK], (1, 1))
            peak = jnp.maximum(jnp.max(scores, axis=0, keepdims=True), FLOOR)
            weights = jnp.exp(scores - peak).astype(BF16)
            e_ref[head, :, at : at + CHUNK] = weights
            out = mat(v_ext, weights, (1, 0))
            own = out[head * dim : (head + 1) * dim]
            total = out[dim : dim + 1] if head == 0 else out[0:1]
            live = total > 0.0
            inv = jnp.where(live, 1.0 / jnp.where(live, total, 1.0), 0.0)
            inv_ref[0, head : head + 1, at : at + CHUNK] = inv
            alone = values_t[head * dim : (head + 1) * dim, at : at + CHUNK]
            pieces.append(jnp.where(live, own * inv, alone))
        halves.append(jnp.concatenate(pieces, axis=1))
    o_ref[...] = jnp.transpose(jnp.concatenate(halves, axis=0)).astype(BF16)


def attend(mixed, marks_q, marks_k):
    count, width3 = mixed.shape
    width = width3 // 3
    seq_n = count // SEQ
    dim = width // HEADS
    pairs = HEADS // 2
    span = 2 * dim
    col = lambda shift: pl.BlockSpec((SEQ, span), lambda s, p: (s, p + shift))
    mark = pl.BlockSpec((SEQ, span), lambda s, p: (s, 0))
    return pl.pallas_call(
        partial(attend_kernel, dim=dim),
        name="attend",
        grid=(seq_n, pairs),
        in_specs=[col(0), col(pairs), col(2 * pairs), mark, mark],
        out_specs=[
            pl.BlockSpec((SEQ, span), lambda s, p: (s, p)),
            pl.BlockSpec((2, SEQ, SEQ), lambda s, p: (s * pairs + p, 0, 0)),
            pl.BlockSpec((1, 8, SEQ), lambda s, p: (s * pairs + p, 0, 0)),
        ],
        out_shape=[
            jax.ShapeDtypeStruct((count, width), BF16),
            jax.ShapeDtypeStruct((seq_n * HEADS, SEQ, SEQ), BF16),
            jax.ShapeDtypeStruct((seq_n * pairs, 8, SEQ), F32),
        ],
        cost_estimate=pl.CostEstimate(
            flops=40_000_000_000, transcendentals=0, bytes_accessed=32_000_000
        ),
    )(mixed, mixed, mixed, marks_q, marks_k)


def attend_back_kernel(
    q_ref, k_ref, v_ref, o_ref, g_ref, a_ref, e_ref, inv_ref, dq_ref, dk_ref, dv_ref, *, dim
):
    length = q_ref.shape[0]
    low_lane = lax.broadcasted_iota(jnp.int32, (length, 2 * dim), 1) < dim
    scale = dim**-0.5
    grads = g_ref[...].astype(F32)
    grads_t = jnp.transpose(grads)
    outs_t = jnp.transpose(o_ref[...].astype(F32))
    keys_t = jnp.transpose(k_ref[...].astype(F32)).astype(BF16)
    values = v_ref[...].astype(F32)
    queries = q_ref[...]
    inv = inv_ref[0]
    row_id = lax.broadcasted_iota(jnp.int32, (dim, length), 0)
    dq_halves, dk_halves, dv_halves = [], [], []
    for head in range(2):
        part = slice(head * dim, (head + 1) * dim)
        lanes = low_lane if head == 0 else ~low_lane
        grad_low = (grads_t[part] * inv[head : head + 1]).astype(BF16)
        inner = -jnp.sum(grad_low.astype(F32) * outs_t[part], axis=0, keepdims=True)
        high = inner.astype(BF16).astype(F32)
        rest = inner - high
        mid = rest.astype(BF16).astype(F32)
        last = rest - mid
        extra = jnp.where(
            row_id == 0, high, jnp.where(row_id == 1, mid, jnp.where(row_id == 2, last, 0.0))
        ).astype(BF16)
        right = jnp.concatenate([grad_low, extra] if head == 0 else [extra, grad_low], axis=0)
        v_ext = jnp.where(lanes, values, 1.0).astype(BF16)
        grad_pair = jnp.concatenate([grad_low, grad_low], axis=0)
        d_keys = jnp.zeros((length, 2 * dim), F32)
        d_values = jnp.zeros((length, 2 * dim), F32)
        dq_parts = []
        for at in range(0, length, CHUNK):
            weights = e_ref[head, :, at : at + CHUNK]
            d_probs = mat(v_ext, right[:, at : at + CHUNK], (1, 0))
            d_scores = weights * d_probs.astype(BF16)
            dq_parts.append(mat(keys_t[part], d_scores, (1, 0)))
            d_keys = d_keys + mat(d_scores, queries[at : at + CHUNK], (1, 0))
            d_values = d_values + mat(weights, grad_pair[:, at : at + CHUNK], (1, 1))
        dq_halves.append(jnp.concatenate(dq_parts, axis=1))
        dk_halves.append(d_keys)
        dv_halves.append(d_values)
    dq_ref[...] = (jnp.transpose(jnp.concatenate(dq_halves, axis=0)) * scale).astype(BF16)
    dk_ref[...] = (jnp.where(low_lane, dk_halves[0], dk_halves[1]) * scale).astype(BF16)
    alone = a_ref[:, 0:1].astype(F32) > 0.0
    d_values = jnp.where(low_lane, dv_halves[0], dv_halves[1])
    dv_ref[...] = jnp.where(alone, grads, d_values).astype(BF16)


def attend_back(mixed, outs, grads, marks_q, weights, inv):
    count, width3 = mixed.shape
    width = width3 // 3
    seq_n = count // SEQ
    dim = width // HEADS
    pairs = HEADS // 2
    span = 2 * dim
    col = lambda shift: pl.BlockSpec((SEQ, span), lambda s, p: (s, p + shift))
    return pl.pallas_call(
        partial(attend_back_kernel, dim=dim),
        name="attend_back",
        grid=(seq_n, pairs),
        in_specs=[
            col(0),
            col(pairs),
            col(2 * pairs),
            col(0),
            col(0),
            pl.BlockSpec((SEQ, span), lambda s, p: (s, 0)),
            pl.BlockSpec((2, SEQ, SEQ), lambda s, p: (s * pairs + p, 0, 0)),
            pl.BlockSpec((1, 8, SEQ), lambda s, p: (s * pairs + p, 0, 0)),
        ],
        out_specs=[col(0), col(0), col(0)],
        out_shape=[jax.ShapeDtypeStruct((count, width), BF16)] * 3,
        cost_estimate=pl.CostEstimate(
            flops=60_000_000_000, transcendentals=0, bytes_accessed=36_000_000
        ),
    )(mixed, mixed, mixed, outs, grads, marks_q, weights, inv)


def up_kernel(x_ref, w_ref, b_ref, act_ref, slope_ref):
    pre = mat(x_ref[...], w_ref[...], (1, 0)) + b_ref[...]
    cdf = 0.5 * (1.0 + lax.erf(pre * (0.5**0.5)))
    act_ref[...] = (pre * cdf).astype(BF16)
    density = jnp.exp(pre * pre * -0.5) * 0.3989422804014327
    slope_ref[...] = (cdf + pre * density).astype(BF16)


def up_project(normed_low, up_weight, up_bias):
    count, width = normed_low.shape
    hidden = up_weight.shape[1]
    rows, tile = min(count, 1024), 256
    spec = pl.BlockSpec((rows, tile), lambda r, f: (r, f))
    return pl.pallas_call(
        up_kernel,
        name="up_project",
        grid=(count // rows, hidden // tile),
        in_specs=[
            pl.BlockSpec((rows, width), lambda r, f: (r, 0)),
            pl.BlockSpec((width, tile), lambda r, f: (0, f)),
            pl.BlockSpec((1, tile), lambda r, f: (0, f)),
        ],
        out_specs=[spec, spec],
        out_shape=[jax.ShapeDtypeStruct((count, hidden), BF16)] * 2,
        cost_estimate=pl.CostEstimate(
            flops=20_000_000_000, transcendentals=0, bytes_accessed=20_000_000
        ),
    )(normed_low, up_weight, up_bias[None])


def per_device(
    tokens,
    segments,
    cotangent,
    qkv_weight,
    out_weight,
    up_weight,
    down_weight,
    qv_bias,
    out_bias,
    norm1_gain,
    norm1_shift,
    up_bias,
    down_bias,
    norm2_gain,
    norm2_shift,
):
    count, width = tokens.shape
    (qv_full, out_full, gain_one, shift_one, up_full, down_full, gain_two, shift_two) = (
        fetch_vectors(
            [
                qv_bias,
                out_bias,
                norm1_gain,
                norm1_shift,
                up_bias,
                down_bias,
                norm2_gain,
                norm2_shift,
            ]
        )
    )
    qkv_full = fetch_weight(qkv_weight)
    out_mat = fetch_weight(out_weight)
    up_mat = fetch_weight(up_weight)
    down_mat = fetch_weight(down_weight)

    lane = lax.broadcasted_iota(jnp.int32, (count, 128), 1) % 64
    seg = segments[:, None]
    marks_q = (seg == lane).astype(BF16)
    marks_k = jnp.where((seg == lane) & (lane != 0), 0.0, NEG).astype(BF16)

    tokens_low = tokens.astype(BF16)
    mix_bias = jnp.concatenate([qv_full[:width], jnp.zeros((width,), F32), qv_full[width:]])
    mixed = (mat(tokens_low, qkv_full, (1, 0)) + mix_bias).astype(BF16)
    attn_low, weights, inv = attend(mixed, marks_q, marks_k)
    first_sum = tokens + mat(attn_low, out_mat, (1, 0)) + out_full
    normed, norm_one_pull = jax.vjp(layer_norm, first_sum, gain_one, shift_one)
    normed_low = normed.astype(BF16)
    act_low, slope = up_project(normed_low, up_mat, up_full)
    second_sum = normed + mat(act_low, down_mat, (1, 0)) + down_full
    layer_out, norm_two_pull = jax.vjp(layer_norm, second_sum, gain_two, shift_two)
    live_rows = (segments != 0).astype(F32)[:, None]
    d_second, d_gain_two, d_shift_two = norm_two_pull(cotangent * live_rows)
    d_feed = d_second.astype(BF16)

    grad_down = spread_grad(mat(act_low, d_feed, (0, 0), BF16))
    grad_down_bias = jnp.sum(d_feed.astype(F32), axis=0)
    d_act = mat(d_feed, down_mat, (1, 1))
    d_pre_low = (d_act * slope.astype(F32)).astype(BF16)
    grad_up = spread_grad(mat(normed_low, d_pre_low, (0, 0), BF16))
    grad_up_bias = jnp.sum(d_pre_low.astype(F32), axis=0)
    d_normed = d_second + mat(d_pre_low, up_mat, (1, 1))
    d_first, d_gain_one, d_shift_one = norm_one_pull(d_normed)
    d_branch = d_first.astype(BF16)
    grad_out_bias = jnp.sum(d_branch.astype(F32), axis=0)
    (
        grad_up_bias,
        grad_down_bias,
        d_gain_two,
        d_shift_two,
        grad_out_bias,
        d_gain_one,
        d_shift_one,
    ) = spread_vectors(
        [
            grad_up_bias,
            grad_down_bias,
            d_gain_two,
            d_shift_two,
            grad_out_bias,
            d_gain_one,
            d_shift_one,
        ]
    )
    grad_out = spread_grad(mat(attn_low, d_branch, (0, 0), BF16))
    d_attended = mat(d_branch, out_mat, (1, 1)).astype(BF16)
    dq_low, dk_low, dv_low = attend_back(mixed, attn_low, d_attended, marks_q, weights, inv)
    d_mixed = jnp.concatenate([dq_low, dk_low, dv_low], axis=1)
    grad_qkv = spread_grad(mat(tokens_low, d_mixed, (0, 0), BF16))
    (grad_qv_bias,) = spread_vectors(
        [
            jnp.concatenate(
                [jnp.sum(dq_low.astype(F32), axis=0), jnp.sum(dv_low.astype(F32), axis=0)]
            )
        ]
    )
    token_grad = d_first + mat(d_mixed, qkv_full, (1, 1))
    return (
        layer_out,
        token_grad,
        grad_qkv,
        grad_out,
        grad_up,
        grad_down,
        grad_qv_bias,
        grad_out_bias,
        d_gain_one,
        d_shift_one,
        grad_up_bias,
        grad_down_bias,
        d_gain_two,
        d_shift_two,
    )


def solution(mesh):
    tokens = P(("dp", "row", "col"), None)
    block = P("row", "col")
    vector = P(("row", "col"))
    return jax.shard_map(
        per_device,
        mesh=mesh,
        in_specs=(tokens, P(("dp", "row", "col")), tokens) + (block,) * 4 + (vector,) * 8,
        out_specs=(tokens, tokens) + (block,) * 4 + (vector,) * 8,
        check_vma=False,
    )
```

```python
from functools import partial

import jax
import jax.numpy as jnp
from jax import lax
from jax.experimental import pallas as pl
from jax.experimental.pallas import tpu as pltpu
from jax.sharding import PartitionSpec as P

HEADS = 12
SEQ = 1024
EPS = 1e-05
NEG = -1e30
FLOOR = -1e29

F32 = jnp.float32
BF16 = jnp.bfloat16


def layer_norm(hidden, gain, shift):
    center = hidden - jnp.mean(hidden, axis=-1, keepdims=True)
    spread = jnp.mean(center * center, axis=-1, keepdims=True)
    return center * lax.rsqrt(spread + EPS) * gain + shift


def mat(left, right, dims, kind=F32):
    return lax.dot_general(left, right, ((dims[:1], dims[1:]), ((), ())), preferred_element_type=kind)


def swap(value, axis, step):
    count = lax.axis_size(axis)
    return lax.ppermute(value, axis, [(i, i ^ step) for i in range(count)])


def steps_up(axis):
    count, out, step = lax.axis_size(axis), [], 1
    while step < count:
        out.append(step)
        step *= 2
    return out


def bit_of(axis, step):
    return (lax.axis_index(axis) // step) % 2


def after(value, *tokens):
    return lax.optimization_barrier((value, tokens))[0]


def widen(value, axis, step, at, cover=()):
    other = after(swap(value, axis, step), *cover)
    mine_low = bit_of(axis, step) == 0
    return jnp.where(mine_low, jnp.stack([value, other], at), jnp.stack([other, value], at))


def gather_up(value, axis):
    value = value[None]
    for step in steps_up(axis):
        value = widen(value, axis, step, 0)
        value = value.reshape((-1,) + value.shape[2:])
    return value


def gather_down(value, axis):
    value = value[None]
    for step in steps_up(axis)[::-1]:
        value = widen(value, axis, step, 1)
        value = value.reshape((-1,) + value.shape[2:])
    return value


def split(value, axis, step, at):
    bit = bit_of(axis, step)
    keep = lax.dynamic_index_in_dim(value, bit, at, keepdims=False)
    return keep, lax.dynamic_index_in_dim(value, 1 - bit, at, keepdims=False)


def merge(keep, got):
    return (keep.astype(F32) + got.astype(F32)).astype(keep.dtype)


def halve(value, axis, step, at):
    keep, send = split(value, axis, step, at)
    return merge(keep, swap(send, axis, step))


def scatter_up(value, axis):
    for step in steps_up(axis):
        value = value.reshape((value.shape[0] // 2, 2) + value.shape[1:])
        value = halve(value, axis, step, 1)
    return value[0]


def scatter_down(value, axis):
    for step in steps_up(axis)[::-1]:
        value = value.reshape((2, value.shape[0] // 2) + value.shape[1:])
        value = halve(value, axis, step, 0)
    return value[0]


def own_piece(block):
    rows, cols = block.shape
    dp_n = lax.axis_size("dp")
    return lax.dynamic_index_in_dim(
        block.reshape(2, dp_n, rows // (2 * dp_n), cols), lax.axis_index("dp"), 1, keepdims=False
    )


def gather_dp_step(first, second, index, cover=()):
    ups = steps_up("dp")
    first = widen(first, "dp", ups[-1 - index], 1, cover)
    second = widen(second, "dp", ups[index], 0, cover)
    return first.reshape((-1,) + first.shape[2:]), second.reshape((-1,) + second.shape[2:])


def gather_dp(pair):
    state = (pair[0][None], pair[1][None])
    for index in range(len(steps_up("dp"))):
        state = gather_dp_step(*state, index)
    return state


def rows_of(pair):
    return jnp.stack(pair).reshape(-1, pair[0].shape[-1])


def join_rows(half, cover=()):
    whole = half[None]
    for step in steps_up("row"):
        whole = widen(whole, "row", step, 0, cover)
        whole = whole.reshape((-1,) + whole.shape[2:])
    return whole.reshape(-1, whole.shape[-1])


def scatter_dp_sends(pair, index):
    first, second = pair
    ups = steps_up("dp")
    near, far = ups[index], ups[-1 - index]
    first = first.reshape((first.shape[0] // 2, 2) + first.shape[1:])
    second = second.reshape((2, second.shape[0] // 2) + second.shape[1:])
    return split(first, "dp", near, 1), split(second, "dp", far, 0), near, far


def scatter_dp_merge(state, cover=()):
    (keep_a, send_a), (keep_b, send_b), near, far = state
    got_a = after(swap(send_a, "dp", near), *cover)
    got_b = after(swap(send_b, "dp", far), *cover)
    return merge(keep_a, got_a), merge(keep_b, got_b)


def row_partial(inputs, grads):
    row_n = lax.axis_size("row")
    if row_n != 2:
        whole = mat(inputs, grads, (0, 0), BF16)
        return whole, scatter_down(whole.reshape(row_n, -1, whole.shape[1]), "row")
    size = inputs.shape[1] // 2
    mine = lax.axis_index("row")
    theirs = lax.dynamic_slice_in_dim(inputs, (1 - mine) * size, size, 1)
    send = mat(theirs, grads, (0, 0), BF16)
    own = lax.dynamic_slice_in_dim(inputs, mine * size, size, 1)
    return send, (mat(own, after(grads, send), (0, 0)) + swap(send, "row", 1).astype(F32)).astype(BF16)


def fold(block, rows):
    return jnp.transpose(block.reshape(-1, rows, block.shape[1]), (1, 0, 2)).reshape(rows, -1)


def unfold(block, cols):
    rows = block.shape[0]
    return jnp.transpose(block.reshape(rows, -1, cols), (1, 0, 2)).reshape(-1, cols)


def to_cols(pair, widths):
    col_n = lax.axis_size("col")
    out, at = [], 0
    for width, groups in widths:
        part = pair[:, :, at : at + groups * width]
        part = part.reshape(part.shape[:2] + (groups, col_n, width // col_n))
        part = jnp.transpose(part, (3, 0, 1, 2, 4))
        out.append(part.reshape(part.shape[:3] + (-1,)))
        at += groups * width
    return jnp.concatenate(out, axis=-1)


def from_cols(wide, widths):
    col_n = lax.axis_size("col")
    out, at = [], 0
    for width, groups in widths:
        own = groups * width // col_n
        part = wide[..., at : at + own]
        part = part.reshape(part.shape[:3] + (groups, width // col_n))
        part = jnp.transpose(part, (1, 2, 3, 0, 4))
        out.append(part.reshape(part.shape[:2] + (-1,)))
        at += own
    return jnp.concatenate(out, axis=-1)


def fetch_vectors(parts):
    sizes = [p.shape[0] for p in parts]
    flat = gather_up(gather_down(jnp.concatenate(parts), "col"), "row")
    flat = flat.reshape(-1, flat.shape[-1])
    out, at = [], 0
    for size in sizes:
        out.append(flat[:, at : at + size].reshape(-1).astype(F32))
        at += size
    return out


def spread_vectors(parts):
    row_n, col_n = lax.axis_size("row"), lax.axis_size("col")
    blocks = row_n * col_n
    flat = jnp.concatenate([p.reshape(blocks, -1) for p in parts], axis=1)
    flat = flat.reshape(row_n, col_n, -1)
    flat = scatter_down(flat, "row")
    flat = scatter_up(flat, "col")
    for step in steps_up("dp"):
        flat = flat + swap(flat, "dp", step)
    out, at = [], 0
    for p in parts:
        size = p.shape[0] // blocks
        out.append(flat[at : at + size])
        at += size
    return out


CHUNK = 256
PARTS = ((0, 2), (2, 3), (5, 1))


def attend_kernel(q_ref, k_ref, v_ref, a_ref, b_ref, o_ref, e_ref, inv_ref, *, dim):
    length = q_ref.shape[0]
    low_lane = lax.broadcasted_iota(jnp.int32, (length, 2 * dim), 1) < dim
    low_row = lax.broadcasted_iota(jnp.int32, (2 * dim, length), 0) < dim
    queries = q_ref[...].astype(F32) * (dim**-0.5)
    keys = k_ref[...].astype(F32)
    marks_q = a_ref[...].astype(F32)
    marks_k = b_ref[...].astype(F32)
    values_t = jnp.transpose(v_ref[...].astype(F32))
    inv_ref[...] = jnp.zeros(inv_ref.shape, F32)
    halves = []
    for head in range(2):
        lanes = low_lane if head == 0 else ~low_lane
        rows = low_row if head == 0 else ~low_row
        q_ext = jnp.where(lanes, queries, marks_q).astype(BF16)
        k_ext = jnp.where(lanes, keys, marks_k).astype(BF16)
        v_ext = jnp.where(rows, values_t, 1.0).astype(BF16)
        pieces = []
        for at in range(0, length, CHUNK):
            scores = mat(k_ext, q_ext[at : at + CHUNK], (1, 1))
            peak = jnp.maximum(jnp.max(scores, axis=0, keepdims=True), FLOOR)
            weights = jnp.exp(scores - peak).astype(BF16)
            e_ref[head, :, at : at + CHUNK] = weights
            out = mat(v_ext, weights, (1, 0))
            own = out[head * dim : (head + 1) * dim]
            total = out[dim : dim + 1] if head == 0 else out[0:1]
            live = total > 0.0
            inv = jnp.where(live, 1.0 / jnp.where(live, total, 1.0), 0.0)
            inv_ref[0, head : head + 1, at : at + CHUNK] = inv
            alone = values_t[head * dim : (head + 1) * dim, at : at + CHUNK]
            pieces.append(jnp.where(live, own * inv, alone))
        halves.append(jnp.concatenate(pieces, axis=1))
    o_ref[...] = jnp.transpose(jnp.concatenate(halves, axis=0)).astype(BF16)


def attend(mixed, marks_q, marks_k, first, part):
    count, width3 = mixed.shape
    width = width3 // 3
    seq_n = count // SEQ
    dim = width // HEADS
    pairs = HEADS // 2
    span = 2 * dim
    col = lambda shift: pl.BlockSpec((SEQ, span), lambda s, p: (s, p + first + shift))
    mark = pl.BlockSpec((SEQ, span), lambda s, p: (s, 0))
    return pl.pallas_call(
        partial(attend_kernel, dim=dim),
        name="attend",
        grid=(seq_n, part),
        in_specs=[col(0), col(pairs), col(2 * pairs), mark, mark],
        out_specs=[
            pl.BlockSpec((SEQ, span), lambda s, p: (s, p)),
            pl.BlockSpec((2, SEQ, SEQ), lambda s, p: (s * part + p, 0, 0)),
            pl.BlockSpec((1, 8, SEQ), lambda s, p: (s * part + p, 0, 0)),
        ],
        out_shape=[
            jax.ShapeDtypeStruct((count, part * span), BF16),
            jax.ShapeDtypeStruct((seq_n * part * 2, SEQ, SEQ), BF16),
            jax.ShapeDtypeStruct((seq_n * part, 8, SEQ), F32),
        ],
        cost_estimate=pl.CostEstimate(
            flops=7_000_000_000 * part, transcendentals=0, bytes_accessed=5_000_000 * part
        ),
    )(mixed, mixed, mixed, marks_q, marks_k)


def attend_back_kernel(
    q_ref, k_ref, v_ref, o_ref, g_ref, a_ref, e_ref, inv_ref, dq_ref, dk_ref, dv_ref, *, dim
):
    length = q_ref.shape[0]
    low_lane = lax.broadcasted_iota(jnp.int32, (length, 2 * dim), 1) < dim
    scale = dim**-0.5
    grads = g_ref[...].astype(F32)
    grads_t = jnp.transpose(grads)
    outs_t = jnp.transpose(o_ref[...].astype(F32))
    keys_t = jnp.transpose(k_ref[...].astype(F32)).astype(BF16)
    values = v_ref[...].astype(F32)
    queries = q_ref[...]
    inv = inv_ref[0]
    row_id = lax.broadcasted_iota(jnp.int32, (dim, length), 0)
    dq_halves, dk_halves, dv_halves = [], [], []
    for head in range(2):
        part = slice(head * dim, (head + 1) * dim)
        lanes = low_lane if head == 0 else ~low_lane
        grad_low = (grads_t[part] * inv[head : head + 1]).astype(BF16)
        inner = -jnp.sum(grad_low.astype(F32) * outs_t[part], axis=0, keepdims=True)
        high = inner.astype(BF16).astype(F32)
        rest = inner - high
        mid = rest.astype(BF16).astype(F32)
        last = rest - mid
        extra = jnp.where(
            row_id == 0, high, jnp.where(row_id == 1, mid, jnp.where(row_id == 2, last, 0.0))
        ).astype(BF16)
        right = jnp.concatenate([grad_low, extra] if head == 0 else [extra, grad_low], axis=0)
        v_ext = jnp.where(lanes, values, 1.0).astype(BF16)
        grad_pair = jnp.concatenate([grad_low, grad_low], axis=0)
        d_keys = jnp.zeros((length, 2 * dim), F32)
        d_values = jnp.zeros((length, 2 * dim), F32)
        dq_parts = []
        for at in range(0, length, CHUNK):
            weights = e_ref[head, :, at : at + CHUNK]
            d_probs = mat(v_ext, right[:, at : at + CHUNK], (1, 0))
            d_scores = weights * d_probs.astype(BF16)
            dq_parts.append(mat(keys_t[part], d_scores, (1, 0)))
            d_keys = d_keys + mat(d_scores, queries[at : at + CHUNK], (1, 0))
            d_values = d_values + mat(weights, grad_pair[:, at : at + CHUNK], (1, 1))
        dq_halves.append(jnp.concatenate(dq_parts, axis=1))
        dk_halves.append(d_keys)
        dv_halves.append(d_values)
    dq_ref[...] = (jnp.transpose(jnp.concatenate(dq_halves, axis=0)) * scale).astype(BF16)
    dk_ref[...] = (jnp.where(low_lane, dk_halves[0], dk_halves[1]) * scale).astype(BF16)
    alone = a_ref[:, 0:1].astype(F32) > 0.0
    d_values = jnp.where(low_lane, dv_halves[0], dv_halves[1])
    dv_ref[...] = jnp.where(alone, grads, d_values).astype(BF16)


def attend_back(mixed, outs, grads, marks_q, weights, inv, first, part):
    count, width3 = mixed.shape
    width = width3 // 3
    seq_n = count // SEQ
    dim = width // HEADS
    pairs = HEADS // 2
    span = 2 * dim
    col = lambda shift: pl.BlockSpec((SEQ, span), lambda s, p: (s, p + first + shift))
    own = pl.BlockSpec((SEQ, span), lambda s, p: (s, p))
    return pl.pallas_call(
        partial(attend_back_kernel, dim=dim),
        name="attend_back",
        grid=(seq_n, part),
        in_specs=[
            col(0),
            col(pairs),
            col(2 * pairs),
            own,
            col(0),
            pl.BlockSpec((SEQ, span), lambda s, p: (s, 0)),
            pl.BlockSpec((2, SEQ, SEQ), lambda s, p: (s * part + p, 0, 0)),
            pl.BlockSpec((1, 8, SEQ), lambda s, p: (s * part + p, 0, 0)),
        ],
        out_specs=[own, own, own],
        out_shape=[jax.ShapeDtypeStruct((count, part * span), BF16)] * 3,
        cost_estimate=pl.CostEstimate(
            flops=7_000_000_000 * part, transcendentals=0, bytes_accessed=6_000_000 * part
        ),
    )(mixed, mixed, mixed, outs, grads, marks_q, weights, inv)


def up_kernel(x_ref, w_ref, b_ref, act_ref, slope_ref):
    pre = mat(x_ref[...], w_ref[...], (1, 0)) + b_ref[...]
    cdf = 0.5 * (1.0 + lax.erf(pre * (0.5**0.5)))
    act_ref[...] = (pre * cdf).astype(BF16)
    density = jnp.exp(pre * pre * -0.5) * 0.3989422804014327
    slope_ref[...] = (cdf + pre * density).astype(BF16)


def up_project(normed_low, up_weight, up_bias):
    count, width = normed_low.shape
    hidden = up_weight.shape[1]
    rows, tile = min(count, 1024), 256
    spec = pl.BlockSpec((rows, tile), lambda r, f: (r, f))
    return pl.pallas_call(
        up_kernel,
        name="up_project",
        grid=(count // rows, hidden // tile),
        in_specs=[
            pl.BlockSpec((rows, width), lambda r, f: (r, 0)),
            pl.BlockSpec((width, tile), lambda r, f: (0, f)),
            pl.BlockSpec((1, tile), lambda r, f: (0, f)),
        ],
        out_specs=[spec, spec],
        out_shape=[jax.ShapeDtypeStruct((count, hidden), BF16)] * 2,
        cost_estimate=pl.CostEstimate(
            flops=20_000_000_000, transcendentals=0, bytes_accessed=20_000_000
        ),
    )(normed_low, up_weight, up_bias[None])


def per_device(
    tokens,
    segments,
    cotangent,
    qkv_weight,
    out_weight,
    up_weight,
    down_weight,
    qv_bias,
    out_bias,
    norm1_gain,
    norm1_shift,
    up_bias,
    down_bias,
    norm2_gain,
    norm2_shift,
):
    count, width = tokens.shape
    (qv_full, out_full, gain_one, shift_one, up_full, down_full, gain_two, shift_two) = (
        fetch_vectors(
            [
                qv_bias,
                out_bias,
                norm1_gain,
                norm1_shift,
                up_bias,
                down_bias,
                norm2_gain,
                norm2_shift,
            ]
        )
    )
    rows, ff = up_weight.shape[0], down_weight.shape[0] // up_weight.shape[0]
    col_n = lax.axis_size("col")
    hidden = up_weight.shape[1] * col_n
    wide_ffn = [(hidden, 1), (width, ff), (width, 1)]
    qkv_cols = gather_down(own_piece(qkv_weight), "col")
    qkv_full = join_rows(rows_of(gather_dp(from_cols(qkv_cols, [(3 * width, 1)]))))
    packed = jnp.concatenate([up_weight, fold(down_weight, rows), out_weight], axis=1)
    ffn_pair = from_cols(gather_down(after(own_piece(packed), qkv_cols), "col"), wide_ffn)

    lane = lax.broadcasted_iota(jnp.int32, (count, 128), 1) % 64
    seg = segments[:, None]
    marks_q = (seg == lane).astype(BF16)
    marks_k = jnp.where((seg == lane) & (lane != 0), 0.0, NEG).astype(BF16)

    tokens_low = tokens.astype(BF16)
    mix_bias = jnp.concatenate([qv_full[:width], jnp.zeros((width,), F32), qv_full[width:]])
    mixed = (mat(tokens_low, qkv_full, (1, 0)) + mix_bias).astype(BF16)
    dp_steps = len(steps_up("dp"))
    kept, ffn_now = [], (ffn_pair[0][None], ffn_pair[1][None])
    for index, (first, part) in enumerate(PARTS):
        kept.append(attend(after(mixed, ffn_now), marks_q, marks_k, first, part))
        if index < dp_steps:
            ffn_now = gather_dp_step(*ffn_now, index, (kept[-1][2],))
        if index == dp_steps - 1:
            ffn_half = rows_of(ffn_now)
            ffn_now = (
                ffn_half[:, :hidden],
                unfold(ffn_half[:, hidden : hidden + ff * width], width),
                ffn_half[:, hidden + ff * width :],
            )
    up_mat, down_mat, out_mat = (join_rows(m, (kept[-1][2],)) for m in ffn_now)
    attn_low = jnp.concatenate([k[0] for k in kept], axis=1)
    first_sum = tokens + mat(attn_low, out_mat, (1, 0)) + out_full
    normed, norm_one_pull = jax.vjp(layer_norm, first_sum, gain_one, shift_one)
    normed_low = normed.astype(BF16)
    act_low, slope = up_project(normed_low, up_mat, up_full)
    second_sum = normed + mat(act_low, down_mat, (1, 0)) + down_full
    layer_out, norm_two_pull = jax.vjp(layer_norm, second_sum, gain_two, shift_two)
    live_rows = (segments != 0).astype(F32)[:, None]
    d_second, d_gain_two, d_shift_two = norm_two_pull(cotangent * live_rows)
    d_feed = d_second.astype(BF16)

    dp_n = lax.axis_size("dp")
    down_send, down_half = row_partial(act_low, d_feed)
    grad_down_bias = jnp.sum(d_feed.astype(F32), axis=0)
    d_act = mat(d_feed, down_mat, (1, 1))
    d_pre_low = (d_act * slope.astype(F32)).astype(BF16)
    up_send, up_half = row_partial(normed_low, d_pre_low)
    grad_up_bias = jnp.sum(d_pre_low.astype(F32), axis=0)
    d_normed = d_second + mat(after(d_pre_low, down_send, up_send), up_mat, (1, 1))
    d_first, d_gain_one, d_shift_one = norm_one_pull(d_normed)
    d_branch = d_first.astype(BF16)
    grad_out_bias = jnp.sum(d_branch.astype(F32), axis=0)
    d_attended = mat(d_branch, out_mat, (1, 1)).astype(BF16)

    half = jnp.concatenate([up_half, fold(down_half, rows)], axis=1)
    half = half.reshape(2, dp_n, -1, half.shape[1])
    pair, results = (half[0], half[1]), {}

    def back_part(which, gate):
        first, part = PARTS[which]
        attn_part, weights, inv = kept[which]
        results[which] = attend_back(
            mixed, attn_part, after(d_attended, gate), marks_q, weights, inv, first, part
        )
        return (results[which][0],)

    for index in range(dp_steps):
        state = scatter_dp_sends(pair, index)
        pair = scatter_dp_merge(state, back_part((1, 0)[index], state[:2]))
    ffn_cols = to_cols(jnp.stack([pair[0][0], pair[1][0]]), wide_ffn[:2])
    near = steps_up("col")[0]
    keep, send = split(ffn_cols.reshape((-1, 2) + ffn_cols.shape[1:]), "col", near, 1)
    ffn_cols = merge(keep, after(swap(send, "col", near), *back_part(2, send)))
    dq_low, dk_low, dv_low = (
        jnp.concatenate([results[w][i] for w in range(len(PARTS))], axis=1) for i in range(3)
    )
    d_mixed = jnp.concatenate([dq_low, dk_low, dv_low], axis=1)
    out_send, out_half = row_partial(attn_low, d_branch)
    qkv_send, qkv_half = row_partial(tokens_low, d_mixed)
    token_grad = d_first + mat(after(d_mixed, qkv_send), qkv_full, (1, 1))

    for far in steps_up("col")[1:]:
        ffn_cols = halve(ffn_cols.reshape((-1, 2) + ffn_cols.shape[1:]), "col", far, 1)
    ffn_grad = rows_of(gather_dp(ffn_cols[0]))
    grad_up = ffn_grad[:, : hidden // col_n].astype(F32)
    grad_down = unfold(ffn_grad[:, hidden // col_n :], width // col_n).astype(F32)
    half = jnp.concatenate([qkv_half, out_half], axis=1)
    half = half.reshape(2, dp_n, -1, half.shape[1])
    pair = (half[0], half[1])
    for index in range(dp_steps):
        pair = scatter_dp_merge(scatter_dp_sends(pair, index))
    attn_cols = to_cols(jnp.stack([pair[0][0], pair[1][0]]), [(3 * width, 1), (width, 1)])
    attn_grad = rows_of(gather_dp(scatter_up(attn_cols, "col")))
    grad_qkv = attn_grad[:, : 3 * width // col_n].astype(F32)
    grad_out = attn_grad[:, 3 * width // col_n :].astype(F32)
    grad_qv_bias = jnp.concatenate(
        [jnp.sum(dq_low.astype(F32), axis=0), jnp.sum(dv_low.astype(F32), axis=0)]
    )
    (
        grad_qv_bias,
        grad_up_bias,
        grad_down_bias,
        d_gain_two,
        d_shift_two,
        grad_out_bias,
        d_gain_one,
        d_shift_one,
    ) = spread_vectors(
        [
            after(grad_qv_bias, qkv_send),
            grad_up_bias,
            grad_down_bias,
            d_gain_two,
            d_shift_two,
            grad_out_bias,
            d_gain_one,
            d_shift_one,
        ]
    )
    return (
        layer_out,
        token_grad,
        grad_qkv,
        grad_out,
        grad_up,
        grad_down,
        grad_qv_bias,
        grad_out_bias,
        d_gain_one,
        d_shift_one,
        grad_up_bias,
        grad_down_bias,
        d_gain_two,
        d_shift_two,
    )


def solution(mesh):
    tokens = P(("dp", "row", "col"), None)
    block = P("row", "col")
    vector = P(("row", "col"))
    return jax.shard_map(
        per_device,
        mesh=mesh,
        in_specs=(tokens, P(("dp", "row", "col")), tokens) + (block,) * 4 + (vector,) * 8,
        out_specs=(tokens, tokens) + (block,) * 4 + (vector,) * 8,
        check_vma=False,
    )
```

```python
from functools import partial

import jax
import jax.numpy as jnp
from jax import lax
from jax.experimental import pallas as pl
from jax.experimental.pallas import tpu as pltpu
from jax.sharding import PartitionSpec as P

HEADS = 12
SEQ = 1024
EPS = 1e-05
NEG = -1e30
FLOOR = -1e29

F32 = jnp.float32
BF16 = jnp.bfloat16


def layer_norm(hidden, gain, shift):
    center = hidden - jnp.mean(hidden, axis=-1, keepdims=True)
    spread = jnp.mean(center * center, axis=-1, keepdims=True)
    return center * lax.rsqrt(spread + EPS) * gain + shift


def mat(left, right, dims, kind=F32):
    return lax.dot_general(left, right, ((dims[:1], dims[1:]), ((), ())), preferred_element_type=kind)


def swap(value, axis, step):
    count = lax.axis_size(axis)
    return lax.ppermute(value, axis, [(i, i ^ step) for i in range(count)])


def steps_up(axis):
    count, out, step = lax.axis_size(axis), [], 1
    while step < count:
        out.append(step)
        step *= 2
    return out


def bit_of(axis, step):
    return (lax.axis_index(axis) // step) % 2


def after(value, *tokens):
    return lax.optimization_barrier((value, tokens))[0]


def tie(*values):
    return lax.optimization_barrier(values)


def widen(value, axis, step, at, cover=()):
    other = after(swap(value, axis, step), *cover)
    mine_low = bit_of(axis, step) == 0
    return jnp.where(mine_low, jnp.stack([value, other], at), jnp.stack([other, value], at))


def gather_up(value, axis):
    value = value[None]
    for step in steps_up(axis):
        value = widen(value, axis, step, 0)
        value = value.reshape((-1,) + value.shape[2:])
    return value


def gather_down(value, axis):
    value = value[None]
    for step in steps_up(axis)[::-1]:
        value = widen(value, axis, step, 1)
        value = value.reshape((-1,) + value.shape[2:])
    return value


def split(value, axis, step, at):
    bit = bit_of(axis, step)
    keep = lax.dynamic_index_in_dim(value, bit, at, keepdims=False)
    return keep, lax.dynamic_index_in_dim(value, 1 - bit, at, keepdims=False)


def merge(keep, got):
    return (keep.astype(F32) + got.astype(F32)).astype(keep.dtype)


def halve(value, axis, step, at):
    keep, send = split(value, axis, step, at)
    return merge(keep, swap(send, axis, step))


def scatter_up(value, axis):
    for step in steps_up(axis):
        value = value.reshape((value.shape[0] // 2, 2) + value.shape[1:])
        value = halve(value, axis, step, 1)
    return value[0]


def scatter_down(value, axis):
    for step in steps_up(axis)[::-1]:
        value = value.reshape((2, value.shape[0] // 2) + value.shape[1:])
        value = halve(value, axis, step, 0)
    return value[0]


def own_piece(block):
    rows, cols = block.shape
    dp_n = lax.axis_size("dp")
    return lax.dynamic_index_in_dim(
        block.reshape(2, dp_n, rows // (2 * dp_n), cols), lax.axis_index("dp"), 1, keepdims=False
    )


def gather_dp_step(first, second, index, cover=()):
    ups = steps_up("dp")
    first = widen(first, "dp", ups[-1 - index], 1, cover)
    second = widen(second, "dp", ups[index], 0, cover)
    return first.reshape((-1,) + first.shape[2:]), second.reshape((-1,) + second.shape[2:])


def gather_dp(pair):
    state = (pair[0][None], pair[1][None])
    for index in range(len(steps_up("dp"))):
        state = gather_dp_step(*state, index)
    return state


def rows_of(pair):
    return jnp.stack(pair).reshape(-1, pair[0].shape[-1])


def join_rows(half, cover=()):
    whole = half[None]
    for step in steps_up("row"):
        whole = widen(whole, "row", step, 0, cover)
        whole = whole.reshape((-1,) + whole.shape[2:])
    return whole.reshape(-1, whole.shape[-1])


def scatter_dp_sends(pair, index):
    first, second = pair
    ups = steps_up("dp")
    near, far = ups[index], ups[-1 - index]
    first = first.reshape((first.shape[0] // 2, 2) + first.shape[1:])
    second = second.reshape((2, second.shape[0] // 2) + second.shape[1:])
    return split(first, "dp", near, 1), split(second, "dp", far, 0), near, far


def scatter_dp_merge(state, cover=()):
    (keep_a, send_a), (keep_b, send_b), near, far = state
    got_a = after(swap(send_a, "dp", near), *cover)
    got_b = after(swap(send_b, "dp", far), *cover)
    return merge(keep_a, got_a), merge(keep_b, got_b)


def row_partial(inputs, grads):
    row_n = lax.axis_size("row")
    if row_n != 2:
        whole = mat(inputs, grads, (0, 0), BF16)
        return whole, scatter_down(whole.reshape(row_n, -1, whole.shape[1]), "row")
    size = inputs.shape[1] // 2
    mine = lax.axis_index("row")
    theirs = lax.dynamic_slice_in_dim(inputs, (1 - mine) * size, size, 1)
    send = mat(theirs, grads, (0, 0), BF16)
    own = lax.dynamic_slice_in_dim(inputs, mine * size, size, 1)
    return send, (mat(own, after(grads, send), (0, 0)) + swap(send, "row", 1).astype(F32)).astype(BF16)


def fold(block, rows):
    return jnp.transpose(block.reshape(-1, rows, block.shape[1]), (1, 0, 2)).reshape(rows, -1)


def unfold(block, cols):
    rows = block.shape[0]
    return jnp.transpose(block.reshape(rows, -1, cols), (1, 0, 2)).reshape(-1, cols)


def to_cols(pair, widths):
    col_n = lax.axis_size("col")
    out, at = [], 0
    for width, groups in widths:
        part = pair[:, :, at : at + groups * width]
        part = part.reshape(part.shape[:2] + (groups, col_n, width // col_n))
        part = jnp.transpose(part, (3, 0, 1, 2, 4))
        out.append(part.reshape(part.shape[:3] + (-1,)))
        at += groups * width
    return jnp.concatenate(out, axis=-1)


def from_cols(wide, widths):
    col_n = lax.axis_size("col")
    out, at = [], 0
    for width, groups in widths:
        own = groups * width // col_n
        part = wide[..., at : at + own]
        part = part.reshape(part.shape[:3] + (groups, width // col_n))
        part = jnp.transpose(part, (1, 2, 3, 0, 4))
        out.append(part.reshape(part.shape[:2] + (-1,)))
        at += own
    return jnp.concatenate(out, axis=-1)


def fetch_vectors(parts):
    sizes = [p.shape[0] for p in parts]
    flat = gather_up(gather_down(jnp.concatenate(parts), "col"), "row")
    flat = flat.reshape(-1, flat.shape[-1])
    out, at = [], 0
    for size in sizes:
        out.append(flat[:, at : at + size].reshape(-1).astype(F32))
        at += size
    return out


def spread_vectors(parts):
    row_n, col_n = lax.axis_size("row"), lax.axis_size("col")
    blocks = row_n * col_n
    flat = jnp.concatenate([p.reshape(blocks, -1) for p in parts], axis=1)
    flat = flat.reshape(row_n, col_n, -1)
    flat = scatter_down(flat, "row")
    flat = scatter_up(flat, "col")
    for step in steps_up("dp"):
        flat = flat + swap(flat, "dp", step)
    out, at = [], 0
    for p in parts:
        size = p.shape[0] // blocks
        out.append(flat[at : at + size])
        at += size
    return out


CHUNK = 256
PARTS = ((0, 2), (2, 3), (5, 1))
KEPT = [pl.BlockSpec(memory_space=pl.ANY)]


def attend_kernel(q_ref, k_ref, v_ref, a_ref, b_ref, *refs, dim):
    o_ref, e_ref, inv_ref = refs[-3:]
    length = q_ref.shape[0]
    low_lane = lax.broadcasted_iota(jnp.int32, (length, 2 * dim), 1) < dim
    low_row = lax.broadcasted_iota(jnp.int32, (2 * dim, length), 0) < dim
    queries = q_ref[...].astype(F32) * (dim**-0.5)
    keys = k_ref[...].astype(F32)
    marks_q = a_ref[...].astype(F32)
    marks_k = b_ref[...].astype(F32)
    values_t = jnp.transpose(v_ref[...].astype(F32))
    inv_ref[...] = jnp.zeros(inv_ref.shape, F32)
    halves = []
    for head in range(2):
        lanes = low_lane if head == 0 else ~low_lane
        rows = low_row if head == 0 else ~low_row
        q_ext = jnp.where(lanes, queries, marks_q).astype(BF16)
        k_ext = jnp.where(lanes, keys, marks_k).astype(BF16)
        v_ext = jnp.where(rows, values_t, 1.0).astype(BF16)
        pieces = []
        for at in range(0, length, CHUNK):
            scores = mat(k_ext, q_ext[at : at + CHUNK], (1, 1))
            peak = jnp.maximum(jnp.max(scores, axis=0, keepdims=True), FLOOR)
            weights = jnp.exp(scores - peak).astype(BF16)
            e_ref[head, :, at : at + CHUNK] = weights
            out = mat(v_ext, weights, (1, 0))
            own = out[head * dim : (head + 1) * dim]
            total = out[dim : dim + 1] if head == 0 else out[0:1]
            live = total > 0.0
            inv = jnp.where(live, 1.0 / jnp.where(live, total, 1.0), 0.0)
            inv_ref[0, head : head + 1, at : at + CHUNK] = inv
            alone = values_t[head * dim : (head + 1) * dim, at : at + CHUNK]
            pieces.append(jnp.where(live, own * inv, alone))
        halves.append(jnp.concatenate(pieces, axis=1))
    o_ref[...] = jnp.transpose(jnp.concatenate(halves, axis=0)).astype(BF16)


def attend(mixed, marks_q, marks_k, first, part, so_far):
    count, width3 = mixed.shape
    width = width3 // 3
    seq_n = count // SEQ
    dim = width // HEADS
    pairs = HEADS // 2
    span = 2 * dim
    col = lambda shift: pl.BlockSpec((SEQ, span), lambda s, p: (s, p + first + shift))
    mark = pl.BlockSpec((SEQ, span), lambda s, p: (s, 0))
    return pl.pallas_call(
        partial(attend_kernel, dim=dim),
        name="attend",
        grid=(seq_n, part),
        in_specs=[col(0), col(pairs), col(2 * pairs), mark, mark] + KEPT * len(so_far),
        input_output_aliases={5 + i: i for i in range(len(so_far))},
        out_specs=[
            col(0),
            pl.BlockSpec((2, SEQ, SEQ), lambda s, p: (s * part + p, 0, 0)),
            pl.BlockSpec((1, 8, SEQ), lambda s, p: (s * part + p, 0, 0)),
        ],
        out_shape=[
            jax.ShapeDtypeStruct((count, width), BF16),
            jax.ShapeDtypeStruct((seq_n * part * 2, SEQ, SEQ), BF16),
            jax.ShapeDtypeStruct((seq_n * part, 8, SEQ), F32),
        ],
        cost_estimate=pl.CostEstimate(
            flops=7_000_000_000 * part, transcendentals=0, bytes_accessed=5_000_000 * part
        ),
    )(mixed, mixed, mixed, marks_q, marks_k, *so_far)


def attend_back_kernel(
    q_ref, k_ref, v_ref, o_ref, g_ref, a_ref, e_ref, inv_ref, *refs, dim
):
    dq_ref, dk_ref, dv_ref = refs[-3:]
    length = q_ref.shape[0]
    low_lane = lax.broadcasted_iota(jnp.int32, (length, 2 * dim), 1) < dim
    scale = dim**-0.5
    grads = g_ref[...].astype(F32)
    grads_t = jnp.transpose(grads)
    outs_t = jnp.transpose(o_ref[...].astype(F32))
    keys_t = jnp.transpose(k_ref[...].astype(F32)).astype(BF16)
    values = v_ref[...].astype(F32)
    queries = q_ref[...]
    inv = inv_ref[0]
    row_id = lax.broadcasted_iota(jnp.int32, (dim, length), 0)
    dq_halves, dk_halves, dv_halves = [], [], []
    for head in range(2):
        part = slice(head * dim, (head + 1) * dim)
        lanes = low_lane if head == 0 else ~low_lane
        grad_low = (grads_t[part] * inv[head : head + 1]).astype(BF16)
        inner = -jnp.sum(grad_low.astype(F32) * outs_t[part], axis=0, keepdims=True)
        high = inner.astype(BF16).astype(F32)
        rest = inner - high
        mid = rest.astype(BF16).astype(F32)
        last = rest - mid
        extra = jnp.where(
            row_id == 0, high, jnp.where(row_id == 1, mid, jnp.where(row_id == 2, last, 0.0))
        ).astype(BF16)
        right = jnp.concatenate([grad_low, extra] if head == 0 else [extra, grad_low], axis=0)
        v_ext = jnp.where(lanes, values, 1.0).astype(BF16)
        grad_pair = jnp.concatenate([grad_low, grad_low], axis=0)
        d_keys = jnp.zeros((length, 2 * dim), F32)
        d_values = jnp.zeros((length, 2 * dim), F32)
        dq_parts = []
        for at in range(0, length, CHUNK):
            weights = e_ref[head, :, at : at + CHUNK]
            d_probs = mat(v_ext, right[:, at : at + CHUNK], (1, 0))
            d_scores = weights * d_probs.astype(BF16)
            dq_parts.append(mat(keys_t[part], d_scores, (1, 0)))
            d_keys = d_keys + mat(d_scores, queries[at : at + CHUNK], (1, 0))
            d_values = d_values + mat(weights, grad_pair[:, at : at + CHUNK], (1, 1))
        dq_halves.append(jnp.concatenate(dq_parts, axis=1))
        dk_halves.append(d_keys)
        dv_halves.append(d_values)
    dq_ref[...] = (jnp.transpose(jnp.concatenate(dq_halves, axis=0)) * scale).astype(BF16)
    dk_ref[...] = (jnp.where(low_lane, dk_halves[0], dk_halves[1]) * scale).astype(BF16)
    alone = a_ref[:, 0:1].astype(F32) > 0.0
    d_values = jnp.where(low_lane, dv_halves[0], dv_halves[1])
    dv_ref[...] = jnp.where(alone, grads, d_values).astype(BF16)


def attend_back(mixed, outs, grads, marks_q, weights, inv, first, part, so_far):
    count, width3 = mixed.shape
    width = width3 // 3
    seq_n = count // SEQ
    dim = width // HEADS
    pairs = HEADS // 2
    span = 2 * dim
    col = lambda shift: pl.BlockSpec((SEQ, span), lambda s, p: (s, p + first + shift))
    return pl.pallas_call(
        partial(attend_back_kernel, dim=dim),
        name="attend_back",
        grid=(seq_n, part),
        in_specs=[
            col(0),
            col(pairs),
            col(2 * pairs),
            col(0),
            col(0),
            pl.BlockSpec((SEQ, span), lambda s, p: (s, 0)),
            pl.BlockSpec((2, SEQ, SEQ), lambda s, p: (s * part + p, 0, 0)),
            pl.BlockSpec((1, 8, SEQ), lambda s, p: (s * part + p, 0, 0)),
        ]
        + KEPT * len(so_far),
        input_output_aliases={8 + i: i for i in range(len(so_far))},
        out_specs=[col(0), col(0), col(0)],
        out_shape=[jax.ShapeDtypeStruct((count, width), BF16)] * 3,
        cost_estimate=pl.CostEstimate(
            flops=7_000_000_000 * part, transcendentals=0, bytes_accessed=6_000_000 * part
        ),
    )(mixed, mixed, mixed, outs, grads, marks_q, weights, inv, *so_far)


def up_kernel(x_ref, w_ref, b_ref, act_ref, slope_ref):
    pre = mat(x_ref[...], w_ref[...], (1, 0)) + b_ref[...]
    cdf = 0.5 * (1.0 + lax.erf(pre * (0.5**0.5)))
    act_ref[...] = (pre * cdf).astype(BF16)
    density = jnp.exp(pre * pre * -0.5) * 0.3989422804014327
    slope_ref[...] = (cdf + pre * density).astype(BF16)


def up_project(normed_low, up_weight, up_bias):
    count, width = normed_low.shape
    hidden = up_weight.shape[1]
    rows, tile = min(count, 1024), 256
    spec = pl.BlockSpec((rows, tile), lambda r, f: (r, f))
    return pl.pallas_call(
        up_kernel,
        name="up_project",
        grid=(count // rows, hidden // tile),
        in_specs=[
            pl.BlockSpec((rows, width), lambda r, f: (r, 0)),
            pl.BlockSpec((width, tile), lambda r, f: (0, f)),
            pl.BlockSpec((1, tile), lambda r, f: (0, f)),
        ],
        out_specs=[spec, spec],
        out_shape=[jax.ShapeDtypeStruct((count, hidden), BF16)] * 2,
        cost_estimate=pl.CostEstimate(
            flops=20_000_000_000, transcendentals=0, bytes_accessed=20_000_000
        ),
    )(normed_low, up_weight, up_bias[None])


def per_device(
    tokens,
    segments,
    cotangent,
    qkv_weight,
    out_weight,
    up_weight,
    down_weight,
    qv_bias,
    out_bias,
    norm1_gain,
    norm1_shift,
    up_bias,
    down_bias,
    norm2_gain,
    norm2_shift,
):
    count, width = tokens.shape
    (qv_full, out_full, gain_one, shift_one, up_full, down_full, gain_two, shift_two) = (
        fetch_vectors(
            [
                qv_bias,
                out_bias,
                norm1_gain,
                norm1_shift,
                up_bias,
                down_bias,
                norm2_gain,
                norm2_shift,
            ]
        )
    )
    rows, ff = up_weight.shape[0], down_weight.shape[0] // up_weight.shape[0]
    col_n = lax.axis_size("col")
    hidden = up_weight.shape[1] * col_n
    wide_ffn = [(hidden, 1), (width, ff), (width, 1)]
    qkv_cols = gather_down(own_piece(qkv_weight), "col")
    qkv_full = join_rows(rows_of(gather_dp(from_cols(qkv_cols, [(3 * width, 1)]))))
    packed = jnp.concatenate([up_weight, fold(down_weight, rows), out_weight], axis=1)
    ffn_pair = from_cols(gather_down(after(own_piece(packed), qkv_cols), "col"), wide_ffn)

    lane = lax.broadcasted_iota(jnp.int32, (count, 128), 1) % 64
    seg = segments[:, None]
    marks_q = (seg == lane).astype(BF16)
    marks_k = jnp.where((seg == lane) & (lane != 0), 0.0, NEG).astype(BF16)

    tokens_low = tokens.astype(BF16)
    mix_bias = jnp.concatenate([qv_full[:width], jnp.zeros((width,), F32), qv_full[width:]])
    mixed = (mat(tokens_low, qkv_full, (1, 0)) + mix_bias).astype(BF16)
    dp_steps = len(steps_up("dp"))
    kept, ffn_now = [], (ffn_pair[0][None], ffn_pair[1][None])
    for index, (first, part) in enumerate(PARTS):
        so_far = (kept[-1][0],) if kept else ()
        kept.append(attend(after(mixed, ffn_now), marks_q, marks_k, first, part, so_far))
        if index < dp_steps:
            ffn_now = gather_dp_step(*ffn_now, index, (kept[-1][2],))
        if index == dp_steps - 1:
            ffn_half = rows_of(ffn_now)
            ffn_now = (
                ffn_half[:, :hidden],
                unfold(ffn_half[:, hidden : hidden + ff * width], width),
                ffn_half[:, hidden + ff * width :],
            )
    up_mat, down_mat, out_mat = (join_rows(m, (kept[-1][2],)) for m in ffn_now)
    attn_low = kept[-1][0]
    first_sum = tokens + mat(attn_low, out_mat, (1, 0)) + out_full
    normed, norm_one_pull = jax.vjp(layer_norm, first_sum, gain_one, shift_one)
    normed_low = normed.astype(BF16)
    act_low, slope = up_project(normed_low, up_mat, up_full)
    second_sum = normed + mat(act_low, down_mat, (1, 0)) + down_full
    layer_out, norm_two_pull = jax.vjp(layer_norm, second_sum, gain_two, shift_two)
    live_rows = (segments != 0).astype(F32)[:, None]
    d_second, d_gain_two, d_shift_two = norm_two_pull(cotangent * live_rows)
    d_feed = d_second.astype(BF16)

    dp_n = lax.axis_size("dp")
    down_send, down_half = row_partial(act_low, d_feed)
    grad_down_bias = jnp.sum(d_feed.astype(F32), axis=0)
    d_act = mat(d_feed, down_mat, (1, 1))
    d_pre_low = (d_act * slope.astype(F32)).astype(BF16)
    up_send, up_half = row_partial(normed_low, d_pre_low)
    grad_up_bias = jnp.sum(d_pre_low.astype(F32), axis=0)
    d_normed = d_second + mat(after(d_pre_low, down_send, up_send), up_mat, (1, 1))
    d_first, d_gain_one, d_shift_one = norm_one_pull(d_normed)
    d_branch = d_first.astype(BF16)
    grad_out_bias = jnp.sum(d_branch.astype(F32), axis=0)
    d_attended = mat(d_branch, out_mat, (1, 1)).astype(BF16)

    half = jnp.concatenate([up_half, fold(down_half, rows)], axis=1)
    half = half.reshape(2, dp_n, -1, half.shape[1])
    pair, results = (half[0], half[1]), [()]
    out_send, out_half = row_partial(attn_low, d_branch)

    def back_part(which, gate):
        first, part = PARTS[which]
        _, weights, inv = kept[which]
        grads = after(d_attended, gate)
        so_far = results[-1]
        results.append(
            attend_back(mixed, attn_low, grads, marks_q, weights, inv, first, part, so_far)
        )
        return tuple(results[-1][:1])

    for index in range(dp_steps):
        state = scatter_dp_sends(pair, index)
        pair = scatter_dp_merge(state, back_part((1, 0)[index], (state[:2], (out_send, out_half)[index])))
    ffn_cols = to_cols(jnp.stack([pair[0][0], pair[1][0]]), wide_ffn[:2])
    near = steps_up("col")[0]
    keep, send = split(ffn_cols.reshape((-1, 2) + ffn_cols.shape[1:]), "col", near, 1)
    ffn_cols = merge(keep, after(swap(send, "col", near), *back_part(2, send)))
    dq_low, dk_low, dv_low = results[-1]
    d_mixed = after(jnp.concatenate([dq_low, dk_low, dv_low], axis=1), ffn_cols)
    grad_qv_bias = jnp.concatenate(
        [jnp.sum(dq_low.astype(F32), axis=0), jnp.sum(dv_low.astype(F32), axis=0)]
    )
    _, qkv_half = row_partial(tokens_low, d_mixed)
    half = jnp.concatenate([qkv_half, out_half], axis=1)
    half = half.reshape(2, dp_n, -1, half.shape[1])
    pair = (half[0], half[1])
    for index in range(dp_steps):
        state = scatter_dp_sends(pair, index)
        if index == 0:
            (keep_a, send_a), (keep_b, send_b), near, far = state
            send_a, send_b, late_mixed, grad_qv_bias = tie(send_a, send_b, d_mixed, grad_qv_bias)
            state = (keep_a, send_a), (keep_b, send_b), near, far
        pair = scatter_dp_merge(state)
    token_grad = d_first + mat(late_mixed, qkv_full, (1, 1))
    attn_cols = to_cols(jnp.stack([pair[0][0], pair[1][0]]), [(3 * width, 1), (width, 1)])
    for far in steps_up("col")[1:]:
        ffn_cols = halve(ffn_cols.reshape((-1, 2) + ffn_cols.shape[1:]), "col", far, 1)
    ffn_own, attn_cols = tie(ffn_cols[0], attn_cols)
    ffn_grad = rows_of(gather_dp(ffn_own))
    attn_grad = rows_of(gather_dp(scatter_up(attn_cols, "col")))
    grad_up = ffn_grad[:, : hidden // col_n].astype(F32)
    grad_down = unfold(ffn_grad[:, hidden // col_n :], width // col_n).astype(F32)
    grad_qkv = attn_grad[:, : 3 * width // col_n].astype(F32)
    grad_out = attn_grad[:, 3 * width // col_n :].astype(F32)
    (
        grad_qv_bias,
        grad_up_bias,
        grad_down_bias,
        d_gain_two,
        d_shift_two,
        grad_out_bias,
        d_gain_one,
        d_shift_one,
    ) = spread_vectors(
        [
            grad_qv_bias,
            grad_up_bias,
            grad_down_bias,
            d_gain_two,
            d_shift_two,
            grad_out_bias,
            d_gain_one,
            d_shift_one,
        ]
    )
    return (
        layer_out,
        token_grad,
        grad_qkv,
        grad_out,
        grad_up,
        grad_down,
        grad_qv_bias,
        grad_out_bias,
        d_gain_one,
        d_shift_one,
        grad_up_bias,
        grad_down_bias,
        d_gain_two,
        d_shift_two,
    )


def solution(mesh):
    tokens = P(("dp", "row", "col"), None)
    block = P("row", "col")
    vector = P(("row", "col"))
    return jax.shard_map(
        per_device,
        mesh=mesh,
        in_specs=(tokens, P(("dp", "row", "col")), tokens) + (block,) * 4 + (vector,) * 8,
        out_specs=(tokens, tokens) + (block,) * 4 + (vector,) * 8,
        check_vma=False,
    )
```

```python
from functools import partial

import jax
import jax.numpy as jnp
from jax import lax
from jax.experimental import pallas as pl
from jax.experimental.pallas import tpu as pltpu
from jax.sharding import PartitionSpec as P

HEADS = 12
SEQ = 1024
EPS = 1e-05
NEG = -1e30
FLOOR = -1e29

F32 = jnp.float32
BF16 = jnp.bfloat16


def layer_norm(hidden, gain, shift):
    center = hidden - jnp.mean(hidden, axis=-1, keepdims=True)
    spread = jnp.mean(center * center, axis=-1, keepdims=True)
    return center * lax.rsqrt(spread + EPS) * gain + shift


def mat(left, right, dims, kind=F32):
    return lax.dot_general(left, right, ((dims[:1], dims[1:]), ((), ())), preferred_element_type=kind)


def swap(value, axis, step):
    count = lax.axis_size(axis)
    return lax.ppermute(value, axis, [(i, i ^ step) for i in range(count)])


def steps_up(axis):
    count, out, step = lax.axis_size(axis), [], 1
    while step < count:
        out.append(step)
        step *= 2
    return out


def bit_of(axis, step):
    return (lax.axis_index(axis) // step) % 2


def after(value, *tokens):
    return lax.optimization_barrier((value, tokens))[0]


def tie(*values):
    return lax.optimization_barrier(values)


def widen(value, axis, step, at, cover=()):
    other = after(swap(value, axis, step), *cover)
    mine_low = bit_of(axis, step) == 0
    return jnp.where(mine_low, jnp.stack([value, other], at), jnp.stack([other, value], at))


def gather_up(value, axis):
    value = value[None]
    for step in steps_up(axis):
        value = widen(value, axis, step, 0)
        value = value.reshape((-1,) + value.shape[2:])
    return value


def gather_down(value, axis):
    value = value[None]
    for step in steps_up(axis)[::-1]:
        value = widen(value, axis, step, 1)
        value = value.reshape((-1,) + value.shape[2:])
    return value


def split(value, axis, step, at):
    bit = bit_of(axis, step)
    keep = lax.dynamic_index_in_dim(value, bit, at, keepdims=False)
    return keep, lax.dynamic_index_in_dim(value, 1 - bit, at, keepdims=False)


def merge(keep, got):
    return (keep.astype(F32) + got.astype(F32)).astype(keep.dtype)


def halve(value, axis, step, at):
    keep, send = split(value, axis, step, at)
    return merge(keep, swap(send, axis, step))


def scatter_up(value, axis):
    for step in steps_up(axis):
        value = value.reshape((value.shape[0] // 2, 2) + value.shape[1:])
        value = halve(value, axis, step, 1)
    return value[0]


def scatter_down(value, axis):
    for step in steps_up(axis)[::-1]:
        value = value.reshape((2, value.shape[0] // 2) + value.shape[1:])
        value = halve(value, axis, step, 0)
    return value[0]


def own_piece(block):
    rows, cols = block.shape
    dp_n = lax.axis_size("dp")
    return lax.dynamic_index_in_dim(
        block.reshape(2, dp_n, rows // (2 * dp_n), cols), lax.axis_index("dp"), 1, keepdims=False
    )


def gather_dp_step(first, second, index, cover=()):
    ups = steps_up("dp")
    first = widen(first, "dp", ups[-1 - index], 1, cover)
    second = widen(second, "dp", ups[index], 0, cover)
    return first.reshape((-1,) + first.shape[2:]), second.reshape((-1,) + second.shape[2:])


def gather_dp(pair):
    state = (pair[0][None], pair[1][None])
    for index in range(len(steps_up("dp"))):
        state = gather_dp_step(*state, index)
    return state


def rows_of(pair):
    return jnp.stack(pair).reshape(-1, pair[0].shape[-1])


def join_rows(half, cover=()):
    whole = half[None]
    for step in steps_up("row"):
        whole = widen(whole, "row", step, 0, cover)
        whole = whole.reshape((-1,) + whole.shape[2:])
    return whole.reshape(-1, whole.shape[-1])


def scatter_dp_sends(pair, index):
    first, second = pair
    ups = steps_up("dp")
    near, far = ups[index], ups[-1 - index]
    first = first.reshape((first.shape[0] // 2, 2) + first.shape[1:])
    second = second.reshape((2, second.shape[0] // 2) + second.shape[1:])
    return split(first, "dp", near, 1), split(second, "dp", far, 0), near, far


def scatter_dp_merge(state, cover=()):
    (keep_a, send_a), (keep_b, send_b), near, far = state
    got_a = after(swap(send_a, "dp", near), *cover)
    got_b = after(swap(send_b, "dp", far), *cover)
    return merge(keep_a, got_a), merge(keep_b, got_b)


def row_partial(inputs, grads):
    row_n = lax.axis_size("row")
    if row_n != 2:
        whole = mat(inputs, grads, (0, 0), BF16)
        return whole, scatter_down(whole.reshape(row_n, -1, whole.shape[1]), "row")
    size = inputs.shape[1] // 2
    mine = lax.axis_index("row")
    theirs = lax.dynamic_slice_in_dim(inputs, (1 - mine) * size, size, 1)
    send = mat(theirs, grads, (0, 0), BF16)
    own = lax.dynamic_slice_in_dim(inputs, mine * size, size, 1)
    return send, (mat(own, after(grads, send), (0, 0)) + swap(send, "row", 1).astype(F32)).astype(BF16)


def fold(block, rows):
    return jnp.transpose(block.reshape(-1, rows, block.shape[1]), (1, 0, 2)).reshape(rows, -1)


def unfold(block, cols):
    rows = block.shape[0]
    return jnp.transpose(block.reshape(rows, -1, cols), (1, 0, 2)).reshape(-1, cols)


def to_cols(pair, widths):
    col_n = lax.axis_size("col")
    out, at = [], 0
    for width, groups in widths:
        part = pair[:, :, at : at + groups * width]
        part = part.reshape(part.shape[:2] + (groups, col_n, width // col_n))
        part = jnp.transpose(part, (3, 0, 1, 2, 4))
        out.append(part.reshape(part.shape[:3] + (-1,)))
        at += groups * width
    return jnp.concatenate(out, axis=-1)


def from_cols(wide, widths):
    col_n = lax.axis_size("col")
    out, at = [], 0
    for width, groups in widths:
        own = groups * width // col_n
        part = wide[..., at : at + own]
        part = part.reshape(part.shape[:3] + (groups, width // col_n))
        part = jnp.transpose(part, (1, 2, 3, 0, 4))
        out.append(part.reshape(part.shape[:2] + (-1,)))
        at += own
    return jnp.concatenate(out, axis=-1)


def fetch_vectors(parts):
    sizes = [p.shape[0] for p in parts]
    flat = gather_up(gather_down(jnp.concatenate(parts), "col"), "row")
    flat = flat.reshape(-1, flat.shape[-1])
    out, at = [], 0
    for size in sizes:
        out.append(flat[:, at : at + size].reshape(-1).astype(F32))
        at += size
    return out


def line_up(parts, rows):
    row_n, col_n = lax.axis_size("row"), lax.axis_size("col")
    flat = jnp.concatenate([p.reshape(row_n * col_n, -1) for p in parts], axis=1)
    flat = scatter_down(flat.reshape(row_n, col_n, -1).astype(BF16), "row")
    flat = jnp.transpose(flat.reshape(col_n, -1, 128 // col_n), (1, 0, 2)).reshape(-1, 128)
    return jnp.pad(flat, ((0, rows - flat.shape[0]), (0, 0)))


def take_apart(block, parts):
    blocks = lax.axis_size("row") * lax.axis_size("col")
    sizes = [p.shape[0] // blocks for p in parts]
    flat = block[: sum(sizes) // block.shape[1]].reshape(-1).astype(F32)
    out, at = [], 0
    for size in sizes:
        out.append(flat[at : at + size])
        at += size
    return out


CHUNK = 256
PARTS = ((0, 2), (2, 3), (5, 1))
KEPT = [pl.BlockSpec(memory_space=pl.ANY)]


def attend_kernel(q_ref, k_ref, v_ref, a_ref, b_ref, *refs, dim):
    o_ref, e_ref, inv_ref = refs[-3:]
    length = q_ref.shape[0]
    low_lane = lax.broadcasted_iota(jnp.int32, (length, 2 * dim), 1) < dim
    low_row = lax.broadcasted_iota(jnp.int32, (2 * dim, length), 0) < dim
    queries = q_ref[...].astype(F32) * (dim**-0.5)
    keys = k_ref[...].astype(F32)
    marks_q = a_ref[...].astype(F32)
    marks_k = b_ref[...].astype(F32)
    values_t = jnp.transpose(v_ref[...].astype(F32))
    inv_ref[...] = jnp.zeros(inv_ref.shape, F32)
    halves = []
    for head in range(2):
        lanes = low_lane if head == 0 else ~low_lane
        rows = low_row if head == 0 else ~low_row
        q_ext = jnp.where(lanes, queries, marks_q).astype(BF16)
        k_ext = jnp.where(lanes, keys, marks_k).astype(BF16)
        v_ext = jnp.where(rows, values_t, 1.0).astype(BF16)
        pieces = []
        for at in range(0, length, CHUNK):
            scores = mat(k_ext, q_ext[at : at + CHUNK], (1, 1))
            peak = jnp.maximum(jnp.max(scores, axis=0, keepdims=True), FLOOR)
            weights = jnp.exp(scores - peak).astype(BF16)
            e_ref[head, :, at : at + CHUNK] = weights
            out = mat(v_ext, weights, (1, 0))
            own = out[head * dim : (head + 1) * dim]
            total = out[dim : dim + 1] if head == 0 else out[0:1]
            live = total > 0.0
            inv = jnp.where(live, 1.0 / jnp.where(live, total, 1.0), 0.0)
            inv_ref[0, head : head + 1, at : at + CHUNK] = inv
            alone = values_t[head * dim : (head + 1) * dim, at : at + CHUNK]
            pieces.append(jnp.where(live, own * inv, alone))
        halves.append(jnp.concatenate(pieces, axis=1))
    o_ref[...] = jnp.transpose(jnp.concatenate(halves, axis=0)).astype(BF16)


def attend(mixed, marks_q, marks_k, first, part, so_far):
    count, width3 = mixed.shape
    width = width3 // 3
    seq_n = count // SEQ
    dim = width // HEADS
    pairs = HEADS // 2
    span = 2 * dim
    col = lambda shift: pl.BlockSpec((SEQ, span), lambda s, p: (s, p + first + shift))
    mark = pl.BlockSpec((SEQ, span), lambda s, p: (s, 0))
    return pl.pallas_call(
        partial(attend_kernel, dim=dim),
        name="attend",
        grid=(seq_n, part),
        in_specs=[col(0), col(pairs), col(2 * pairs), mark, mark] + KEPT * len(so_far),
        input_output_aliases={5 + i: i for i in range(len(so_far))},
        out_specs=[
            col(0),
            pl.BlockSpec((2, SEQ, SEQ), lambda s, p: (s * part + p, 0, 0)),
            pl.BlockSpec((1, 8, SEQ), lambda s, p: (s * part + p, 0, 0)),
        ],
        out_shape=[
            jax.ShapeDtypeStruct((count, width), BF16),
            jax.ShapeDtypeStruct((seq_n * part * 2, SEQ, SEQ), BF16),
            jax.ShapeDtypeStruct((seq_n * part, 8, SEQ), F32),
        ],
        cost_estimate=pl.CostEstimate(
            flops=7_000_000_000 * part, transcendentals=0, bytes_accessed=5_000_000 * part
        ),
    )(mixed, mixed, mixed, marks_q, marks_k, *so_far)


def attend_back_kernel(
    q_ref, k_ref, v_ref, o_ref, g_ref, a_ref, e_ref, inv_ref, *refs, dim
):
    dq_ref, dk_ref, dv_ref = refs[-3:]
    length = q_ref.shape[0]
    low_lane = lax.broadcasted_iota(jnp.int32, (length, 2 * dim), 1) < dim
    scale = dim**-0.5
    grads = g_ref[...].astype(F32)
    grads_t = jnp.transpose(grads)
    outs_t = jnp.transpose(o_ref[...].astype(F32))
    keys_t = jnp.transpose(k_ref[...].astype(F32)).astype(BF16)
    values = v_ref[...].astype(F32)
    queries = q_ref[...]
    inv = inv_ref[0]
    row_id = lax.broadcasted_iota(jnp.int32, (dim, length), 0)
    dq_halves, dk_halves, dv_halves = [], [], []
    for head in range(2):
        part = slice(head * dim, (head + 1) * dim)
        lanes = low_lane if head == 0 else ~low_lane
        grad_low = (grads_t[part] * inv[head : head + 1]).astype(BF16)
        inner = -jnp.sum(grad_low.astype(F32) * outs_t[part], axis=0, keepdims=True)
        high = inner.astype(BF16).astype(F32)
        rest = inner - high
        mid = rest.astype(BF16).astype(F32)
        last = rest - mid
        extra = jnp.where(
            row_id == 0, high, jnp.where(row_id == 1, mid, jnp.where(row_id == 2, last, 0.0))
        ).astype(BF16)
        right = jnp.concatenate([grad_low, extra] if head == 0 else [extra, grad_low], axis=0)
        v_ext = jnp.where(lanes, values, 1.0).astype(BF16)
        grad_pair = jnp.concatenate([grad_low, grad_low], axis=0)
        d_keys = jnp.zeros((length, 2 * dim), F32)
        d_values = jnp.zeros((length, 2 * dim), F32)
        dq_parts = []
        for at in range(0, length, CHUNK):
            weights = e_ref[head, :, at : at + CHUNK]
            d_probs = mat(v_ext, right[:, at : at + CHUNK], (1, 0))
            d_scores = weights * d_probs.astype(BF16)
            dq_parts.append(mat(keys_t[part], d_scores, (1, 0)))
            d_keys = d_keys + mat(d_scores, queries[at : at + CHUNK], (1, 0))
            d_values = d_values + mat(weights, grad_pair[:, at : at + CHUNK], (1, 1))
        dq_halves.append(jnp.concatenate(dq_parts, axis=1))
        dk_halves.append(d_keys)
        dv_halves.append(d_values)
    dq_ref[...] = (jnp.transpose(jnp.concatenate(dq_halves, axis=0)) * scale).astype(BF16)
    dk_ref[...] = (jnp.where(low_lane, dk_halves[0], dk_halves[1]) * scale).astype(BF16)
    alone = a_ref[:, 0:1].astype(F32) > 0.0
    d_values = jnp.where(low_lane, dv_halves[0], dv_halves[1])
    dv_ref[...] = jnp.where(alone, grads, d_values).astype(BF16)


def attend_back(mixed, outs, grads, marks_q, weights, inv, first, part, so_far):
    count, width3 = mixed.shape
    width = width3 // 3
    seq_n = count // SEQ
    dim = width // HEADS
    pairs = HEADS // 2
    span = 2 * dim
    col = lambda shift: pl.BlockSpec((SEQ, span), lambda s, p: (s, p + first + shift))
    return pl.pallas_call(
        partial(attend_back_kernel, dim=dim),
        name="attend_back",
        grid=(seq_n, part),
        in_specs=[
            col(0),
            col(pairs),
            col(2 * pairs),
            col(0),
            col(0),
            pl.BlockSpec((SEQ, span), lambda s, p: (s, 0)),
            pl.BlockSpec((2, SEQ, SEQ), lambda s, p: (s * part + p, 0, 0)),
            pl.BlockSpec((1, 8, SEQ), lambda s, p: (s * part + p, 0, 0)),
        ]
        + KEPT * len(so_far),
        input_output_aliases={8 + i: i for i in range(len(so_far))},
        out_specs=[col(0), col(0), col(0)],
        out_shape=[jax.ShapeDtypeStruct((count, width), BF16)] * 3,
        cost_estimate=pl.CostEstimate(
            flops=7_000_000_000 * part, transcendentals=0, bytes_accessed=6_000_000 * part
        ),
    )(mixed, mixed, mixed, outs, grads, marks_q, weights, inv, *so_far)


def up_kernel(x_ref, w_ref, b_ref, act_ref, slope_ref):
    pre = mat(x_ref[...], w_ref[...], (1, 0)) + b_ref[...]
    cdf = 0.5 * (1.0 + lax.erf(pre * (0.5**0.5)))
    act_ref[...] = (pre * cdf).astype(BF16)
    density = jnp.exp(pre * pre * -0.5) * 0.3989422804014327
    slope_ref[...] = (cdf + pre * density).astype(BF16)


def up_project(normed_low, up_weight, up_bias):
    count, width = normed_low.shape
    hidden = up_weight.shape[1]
    rows, tile = min(count, 1024), 256
    spec = pl.BlockSpec((rows, tile), lambda r, f: (r, f))
    return pl.pallas_call(
        up_kernel,
        name="up_project",
        grid=(count // rows, hidden // tile),
        in_specs=[
            pl.BlockSpec((rows, width), lambda r, f: (r, 0)),
            pl.BlockSpec((width, tile), lambda r, f: (0, f)),
            pl.BlockSpec((1, tile), lambda r, f: (0, f)),
        ],
        out_specs=[spec, spec],
        out_shape=[jax.ShapeDtypeStruct((count, hidden), BF16)] * 2,
        cost_estimate=pl.CostEstimate(
            flops=20_000_000_000, transcendentals=0, bytes_accessed=20_000_000
        ),
    )(normed_low, up_weight, up_bias[None])


def piece_spec(block, lane, index, axis_of_piece):
    def place(k, t, own):
        return (0, jnp.where(k == index, lane(t), lane(0)) if axis_of_piece else lane(t))

    return pl.BlockSpec(block, place)


def up_rows_kernel(own_ref, *refs, pieces):
    b_ref, act_ref, slope_ref = refs[2 * pieces :]
    pre = b_ref[...]
    for k in range(pieces):
        pre = pre + mat(refs[k][...], refs[pieces + k][...], (1, 0))
    cdf = 0.5 * (1.0 + lax.erf(pre * (0.5**0.5)))
    act_ref[...] = (pre * cdf).astype(BF16)
    density = jnp.exp(pre * pre * -0.5) * 0.3989422804014327
    slope_ref[...] = (cdf + pre * density).astype(BF16)


def up_rows(own, inputs, packs, bias):
    count = inputs.shape[0]
    rows, hidden, tile = packs[0].shape[0], bias.shape[0], 256
    pieces = len(packs)
    spec = pl.BlockSpec((count, tile), lambda f, own: (0, f))
    xs = [pl.BlockSpec((count, rows), lambda f, own, k=k: (0, own[0] ^ k)) for k in range(pieces)]
    ws = [pl.BlockSpec((rows, tile), lambda f, own: (0, f))] * pieces
    return pl.pallas_call(
        partial(up_rows_kernel, pieces=pieces),
        name="up_rows",
        grid_spec=pltpu.PrefetchScalarGridSpec(
            num_scalar_prefetch=1,
            grid=(hidden // tile,),
            in_specs=xs + ws + [pl.BlockSpec((1, tile), lambda f, own: (0, f))],
            out_specs=[spec, spec],
        ),
        out_shape=[jax.ShapeDtypeStruct((count, hidden), BF16)] * 2,
        cost_estimate=pl.CostEstimate(
            flops=15_000_000_000, transcendentals=0, bytes_accessed=20_000_000
        ),
    )(own, *[inputs] * pieces, *packs, bias[None])


def down_rows_kernel(own_ref, *refs, pieces):
    base_ref, b_ref, out_ref = refs[2 * pieces :]

    @pl.when(pl.program_id(0) == 0)
    def _():
        out_ref[...] = base_ref[...] + b_ref[...]

    total = mat(refs[0][...], refs[pieces][...], (1, 0))
    for k in range(1, pieces):
        total = total + mat(refs[k][...], refs[pieces + k][...], (1, 0))
    out_ref[...] += total


def down_rows(own, inputs, packs, base, bias, lane):
    count, width = base.shape
    rows, pieces = packs[0].shape[0], len(packs)
    groups = inputs.shape[1] // (rows * pieces)
    xs = [
        pl.BlockSpec((count, rows), lambda g, own, k=k: (0, (own[0] ^ k) * groups + g))
        for k in range(pieces)
    ]
    ws = [pl.BlockSpec((rows, width), lambda g, own: (0, lane + g))] * pieces
    return pl.pallas_call(
        partial(down_rows_kernel, pieces=pieces),
        name="down_rows",
        grid_spec=pltpu.PrefetchScalarGridSpec(
            num_scalar_prefetch=1,
            grid=(groups,),
            in_specs=xs
            + ws
            + [
                pl.BlockSpec((count, width), lambda g, own: (0, 0)),
                pl.BlockSpec((1, width), lambda g, own: (0, 0)),
            ],
            out_specs=pl.BlockSpec((count, width), lambda g, own: (0, 0)),
        ),
        out_shape=jax.ShapeDtypeStruct((count, width), F32),
        cost_estimate=pl.CostEstimate(
            flops=7_000_000_000, transcendentals=0, bytes_accessed=17_000_000
        ),
    )(own, *[inputs] * pieces, *packs, base, bias[None])


def pre_back_kernel(own_ref, grad_ref, slope_ref, *refs, pieces):
    out_ref, sum_ref = refs[pieces:]
    for k in range(pieces):

        @pl.when(pl.program_id(0) == k)
        def _():
            d_act = mat(grad_ref[...], refs[k][...], (1, 1))
            d_pre = (d_act * slope_ref[...].astype(F32)).astype(BF16)
            out_ref[...] = d_pre
            sum_ref[...] = jnp.sum(d_pre.astype(F32), axis=0, keepdims=True)


def pre_back(own, grads, slope, packs, lane):
    count, width = grads.shape
    rows, pieces = packs[0].shape[0], len(packs)
    hidden = slope.shape[1]
    groups = hidden // (rows * pieces)
    tile = lambda k, g, own: (0, (own[0] ^ k) * groups + g)
    return pl.pallas_call(
        partial(pre_back_kernel, pieces=pieces),
        name="pre_back",
        grid_spec=pltpu.PrefetchScalarGridSpec(
            num_scalar_prefetch=1,
            grid=(pieces, groups),
            in_specs=[
                pl.BlockSpec((count, width), lambda k, g, own: (0, 0)),
                pl.BlockSpec((count, rows), tile),
            ]
            + [piece_spec((rows, width), lambda t: lane + t, k, True) for k in range(pieces)],
            out_specs=[pl.BlockSpec((count, rows), tile), pl.BlockSpec((1, rows), tile)],
        ),
        out_shape=[
            jax.ShapeDtypeStruct((count, hidden), BF16),
            jax.ShapeDtypeStruct((1, hidden), F32),
        ],
        cost_estimate=pl.CostEstimate(
            flops=7_000_000_000, transcendentals=0, bytes_accessed=18_000_000
        ),
    )(own, grads, slope, *packs)


def normed_back_kernel(own_ref, grad_ref, base_ref, *refs, pieces):
    out_ref = refs[pieces]

    @pl.when(pl.program_id(1) == 0)
    def _():
        out_ref[...] = base_ref[...]

    for k in range(pieces):

        @pl.when(pl.program_id(0) == k)
        def _():
            out_ref[...] += mat(grad_ref[...], refs[k][...], (1, 1))


def normed_back(own, grads, base, packs):
    count, width = base.shape
    rows, pieces = packs[0].shape[0], len(packs)
    hidden = grads.shape[1]
    part = pl.BlockSpec((count, rows), lambda k, t, own: (0, own[0] ^ k))
    return pl.pallas_call(
        partial(normed_back_kernel, pieces=pieces),
        name="normed_back",
        grid_spec=pltpu.PrefetchScalarGridSpec(
            num_scalar_prefetch=1,
            grid=(pieces, hidden // width),
            in_specs=[pl.BlockSpec((count, width), lambda k, t, own: (0, t)), part]
            + [piece_spec((rows, width), lambda t: t, k, True) for k in range(pieces)],
            out_specs=part,
        ),
        out_shape=jax.ShapeDtypeStruct((count, width), F32),
        cost_estimate=pl.CostEstimate(
            flops=7_000_000_000, transcendentals=0, bytes_accessed=18_000_000
        ),
    )(own, grads, base, *packs)


def per_device(
    tokens,
    segments,
    cotangent,
    qkv_weight,
    out_weight,
    up_weight,
    down_weight,
    qv_bias,
    out_bias,
    norm1_gain,
    norm1_shift,
    up_bias,
    down_bias,
    norm2_gain,
    norm2_shift,
):
    count, width = tokens.shape
    (qv_full, out_full, gain_one, shift_one, up_full, down_full, gain_two, shift_two) = (
        fetch_vectors(
            [
                qv_bias,
                out_bias,
                norm1_gain,
                norm1_shift,
                up_bias,
                down_bias,
                norm2_gain,
                norm2_shift,
            ]
        )
    )
    rows, ff = up_weight.shape[0], down_weight.shape[0] // up_weight.shape[0]
    col_n = lax.axis_size("col")
    hidden = up_weight.shape[1] * col_n
    wide_ffn = [(hidden, 1), (width, ff), (width, 1)]
    qkv_cols = gather_down(own_piece(qkv_weight), "col")
    qkv_full = join_rows(rows_of(gather_dp(from_cols(qkv_cols, [(3 * width, 1)]))))
    packed = jnp.concatenate([up_weight, fold(down_weight, rows), out_weight], axis=1)
    ffn_pair = from_cols(gather_down(after(own_piece(packed), qkv_cols), "col"), wide_ffn)

    lane = lax.broadcasted_iota(jnp.int32, (count, 128), 1) % 64
    seg = segments[:, None]
    marks_q = (seg == lane).astype(BF16)
    marks_k = jnp.where((seg == lane) & (lane != 0), 0.0, NEG).astype(BF16)

    tokens_low = tokens.astype(BF16)
    mix_bias = jnp.concatenate([qv_full[:width], jnp.zeros((width,), F32), qv_full[width:]])
    mixed = (mat(tokens_low, qkv_full, (1, 0)) + mix_bias).astype(BF16)
    dp_steps = len(steps_up("dp"))
    kept, ffn_now = [], (ffn_pair[0][None], ffn_pair[1][None])
    for index, (first, part) in enumerate(PARTS):
        so_far = (kept[-1][0],) if kept else ()
        kept.append(attend(after(mixed, ffn_now), marks_q, marks_k, first, part, so_far))
        if index < dp_steps:
            ffn_now = gather_dp_step(*ffn_now, index, (kept[-1][2],))
        if index == dp_steps - 1:
            ffn_half = rows_of(ffn_now)
            ffn_now = ffn_half
    packs = [ffn_half]
    for step in steps_up("row"):
        packs = packs + [after(swap(p, "row", step), kept[-1][2]) for p in packs]
    own_row = lax.axis_index("row")
    direct = rows % 128 == 0 and hidden % width == 0 and hidden == len(packs) * ff * rows
    place = own_row.reshape(1).astype(jnp.int32)

    def natural_rows(parts):
        order = jnp.stack(parts)
        for step in steps_up("row"):
            pairs = order.reshape((-1, 2, step) + order.shape[1:])
            flipped = jnp.where(bit_of("row", step) == 0, pairs, pairs[:, ::-1])
            order = flipped.reshape(order.shape)
        return order.reshape(-1, order.shape[-1])

    out_mat = natural_rows([p[:, hidden + ff * width :] for p in packs])
    if not direct:
        up_mat = natural_rows([p[:, :hidden] for p in packs])
        down_mat = natural_rows([unfold(p[:, hidden : hidden + ff * width], width) for p in packs])
    attn_low = kept[-1][0]
    first_sum = tokens + mat(attn_low, out_mat, (1, 0)) + out_full
    normed, norm_one_pull = jax.vjp(layer_norm, first_sum, gain_one, shift_one)
    normed_low = normed.astype(BF16)
    if direct:
        act_low, slope = up_rows(place, normed_low, packs, up_full)
        second_sum = down_rows(place, act_low, packs, normed, down_full, hidden // width)
    else:
        act_low, slope = up_project(normed_low, up_mat, up_full)
        second_sum = normed + mat(act_low, down_mat, (1, 0)) + down_full
    layer_out, norm_two_pull = jax.vjp(layer_norm, second_sum, gain_two, shift_two)
    live_rows = (segments != 0).astype(F32)[:, None]
    d_second, d_gain_two, d_shift_two = norm_two_pull(cotangent * live_rows)
    d_feed = d_second.astype(BF16)

    dp_n = lax.axis_size("dp")
    down_send, down_half = row_partial(act_low, d_feed)
    grad_down_bias = jnp.sum(d_feed.astype(F32), axis=0)
    if direct:
        d_pre_low, grad_up_bias = pre_back(place, d_feed, slope, packs, hidden // width)
        grad_up_bias = grad_up_bias[0]
    else:
        d_act = mat(d_feed, down_mat, (1, 1))
        d_pre_low = (d_act * slope.astype(F32)).astype(BF16)
        grad_up_bias = jnp.sum(d_pre_low.astype(F32), axis=0)
    up_send, up_half = row_partial(normed_low, d_pre_low)
    late_pre = after(d_pre_low, down_send, up_send)
    if direct:
        d_normed = normed_back(place, late_pre, d_second, packs)
    else:
        d_normed = d_second + mat(late_pre, up_mat, (1, 1))
    d_first, d_gain_one, d_shift_one = norm_one_pull(d_normed)
    d_branch = d_first.astype(BF16)
    grad_out_bias = jnp.sum(d_branch.astype(F32), axis=0)
    d_attended = mat(d_branch, out_mat, (1, 1)).astype(BF16)

    half = jnp.concatenate([up_half, fold(down_half, rows)], axis=1)
    half = half.reshape(2, dp_n, -1, half.shape[1])
    pair, results = (half[0], half[1]), [()]
    out_send, out_half = row_partial(attn_low, d_branch)

    def back_part(which, gate):
        first, part = PARTS[which]
        _, weights, inv = kept[which]
        grads = after(d_attended, gate)
        so_far = results[-1]
        results.append(
            attend_back(mixed, attn_low, grads, marks_q, weights, inv, first, part, so_far)
        )
        return tuple(results[-1][:1])

    for index in range(dp_steps):
        state = scatter_dp_sends(pair, index)
        pair = scatter_dp_merge(state, back_part((1, 0)[index], (state[:2], (out_send, out_half)[index])))
    ffn_cols = to_cols(jnp.stack([pair[0][0], pair[1][0]]), wide_ffn[:2])
    near = steps_up("col")[0]
    keep, send = split(ffn_cols.reshape((-1, 2) + ffn_cols.shape[1:]), "col", near, 1)
    ffn_cols = merge(keep, after(swap(send, "col", near), *back_part(2, send)))
    dq_low, dk_low, dv_low = results[-1]
    d_mixed = after(jnp.concatenate([dq_low, dk_low, dv_low], axis=1), ffn_cols)
    grad_qv_bias = jnp.concatenate(
        [jnp.sum(dq_low.astype(F32), axis=0), jnp.sum(dv_low.astype(F32), axis=0)]
    )
    _, qkv_half = row_partial(tokens_low, d_mixed)
    vectors = [
        grad_qv_bias,
        grad_up_bias,
        grad_down_bias,
        d_gain_two,
        d_shift_two,
        grad_out_bias,
        d_gain_one,
        d_shift_one,
    ]
    half = jnp.concatenate([qkv_half, out_half, line_up(vectors, rows)], axis=1)
    half = half.reshape(2, dp_n, -1, half.shape[1])
    pair = (half[0], half[1])
    for index in range(dp_steps):
        state = scatter_dp_sends(pair, index)
        if index == 0:
            (keep_a, send_a), (keep_b, send_b), near, far = state
            send_a, send_b, late_mixed = tie(send_a, send_b, d_mixed)
            state = (keep_a, send_a), (keep_b, send_b), near, far
        pair = scatter_dp_merge(state)
    token_grad = d_first + mat(late_mixed, qkv_full, (1, 1))
    attn_cols = to_cols(jnp.stack([pair[0][0], pair[1][0]]), [(3 * width, 1), (width, 1), (128, 1)])
    for far in steps_up("col")[1:]:
        ffn_cols = halve(ffn_cols.reshape((-1, 2) + ffn_cols.shape[1:]), "col", far, 1)
    ffn_own, attn_cols = tie(ffn_cols[0], attn_cols)
    ffn_grad = rows_of(gather_dp(ffn_own))
    attn_grad = rows_of(gather_dp(scatter_up(attn_cols, "col")))
    grad_up = ffn_grad[:, : hidden // col_n].astype(F32)
    grad_down = unfold(ffn_grad[:, hidden // col_n :], width // col_n).astype(F32)
    grad_qkv = attn_grad[:, : 3 * width // col_n].astype(F32)
    grad_out = attn_grad[:, 3 * width // col_n : 4 * width // col_n].astype(F32)
    (
        grad_qv_bias,
        grad_up_bias,
        grad_down_bias,
        d_gain_two,
        d_shift_two,
        grad_out_bias,
        d_gain_one,
        d_shift_one,
    ) = take_apart(attn_grad[:, 4 * width // col_n :], vectors)
    return (
        layer_out,
        token_grad,
        grad_qkv,
        grad_out,
        grad_up,
        grad_down,
        grad_qv_bias,
        grad_out_bias,
        d_gain_one,
        d_shift_one,
        grad_up_bias,
        grad_down_bias,
        d_gain_two,
        d_shift_two,
    )


def solution(mesh):
    tokens = P(("dp", "row", "col"), None)
    block = P("row", "col")
    vector = P(("row", "col"))
    return jax.shard_map(
        per_device,
        mesh=mesh,
        in_specs=(tokens, P(("dp", "row", "col")), tokens) + (block,) * 4 + (vector,) * 8,
        out_specs=(tokens, tokens) + (block,) * 4 + (vector,) * 8,
        check_vma=False,
    )
```

```python
from functools import partial

import jax
import jax.numpy as jnp
from jax import lax
from jax.experimental import pallas as pl
from jax.experimental.pallas import tpu as pltpu
from jax.sharding import PartitionSpec as P

HEADS = 12
SEQ = 1024
EPS = 1e-05
NEG = -1e30
FLOOR = -1e29

F32 = jnp.float32
BF16 = jnp.bfloat16


def layer_norm(hidden, gain, shift):
    center = hidden - jnp.mean(hidden, axis=-1, keepdims=True)
    spread = jnp.mean(center * center, axis=-1, keepdims=True)
    return center * lax.rsqrt(spread + EPS) * gain + shift


def mat(left, right, dims, kind=F32):
    return lax.dot_general(left, right, ((dims[:1], dims[1:]), ((), ())), preferred_element_type=kind)


def swap(value, axis, step):
    count = lax.axis_size(axis)
    return lax.ppermute(value, axis, [(i, i ^ step) for i in range(count)])


def steps_up(axis):
    count, out, step = lax.axis_size(axis), [], 1
    while step < count:
        out.append(step)
        step *= 2
    return out


def bit_of(axis, step):
    return (lax.axis_index(axis) // step) % 2


def after(value, *tokens):
    return lax.optimization_barrier((value, tokens))[0]


def tie(*values):
    return lax.optimization_barrier(values)


def widen(value, axis, step, at, cover=()):
    other = after(swap(value, axis, step), *cover)
    mine_low = bit_of(axis, step) == 0
    return jnp.where(mine_low, jnp.stack([value, other], at), jnp.stack([other, value], at))


def gather_up(value, axis):
    value = value[None]
    for step in steps_up(axis):
        value = widen(value, axis, step, 0)
        value = value.reshape((-1,) + value.shape[2:])
    return value


def gather_down(value, axis):
    value = value[None]
    for step in steps_up(axis)[::-1]:
        value = widen(value, axis, step, 1)
        value = value.reshape((-1,) + value.shape[2:])
    return value


def split(value, axis, step, at):
    bit = bit_of(axis, step)
    keep = lax.dynamic_index_in_dim(value, bit, at, keepdims=False)
    return keep, lax.dynamic_index_in_dim(value, 1 - bit, at, keepdims=False)


def merge(keep, got):
    return (keep.astype(F32) + got.astype(F32)).astype(keep.dtype)


def halve(value, axis, step, at):
    keep, send = split(value, axis, step, at)
    return merge(keep, swap(send, axis, step))


def scatter_up(value, axis):
    for step in steps_up(axis):
        value = value.reshape((value.shape[0] // 2, 2) + value.shape[1:])
        value = halve(value, axis, step, 1)
    return value[0]


def scatter_down(value, axis):
    for step in steps_up(axis)[::-1]:
        value = value.reshape((2, value.shape[0] // 2) + value.shape[1:])
        value = halve(value, axis, step, 0)
    return value[0]


def own_piece(block):
    rows, cols = block.shape
    dp_n = lax.axis_size("dp")
    return lax.dynamic_index_in_dim(
        block.reshape(2, dp_n, rows // (2 * dp_n), cols), lax.axis_index("dp"), 1, keepdims=False
    )


def gather_dp_step(first, second, index, cover=()):
    ups = steps_up("dp")
    first = widen(first, "dp", ups[-1 - index], 1, cover)
    second = widen(second, "dp", ups[index], 0, cover)
    return first.reshape((-1,) + first.shape[2:]), second.reshape((-1,) + second.shape[2:])


def gather_dp(pair):
    state = (pair[0][None], pair[1][None])
    for index in range(len(steps_up("dp"))):
        state = gather_dp_step(*state, index)
    return state


def rows_of(pair):
    return jnp.stack(pair).reshape(-1, pair[0].shape[-1])


def join_rows(half, cover=()):
    whole = half[None]
    for step in steps_up("row"):
        whole = widen(whole, "row", step, 0, cover)
        whole = whole.reshape((-1,) + whole.shape[2:])
    return whole.reshape(-1, whole.shape[-1])


def scatter_dp_sends(pair, index):
    first, second = pair
    ups = steps_up("dp")
    near, far = ups[index], ups[-1 - index]
    first = first.reshape((first.shape[0] // 2, 2) + first.shape[1:])
    second = second.reshape((2, second.shape[0] // 2) + second.shape[1:])
    return split(first, "dp", near, 1), split(second, "dp", far, 0), near, far


def scatter_dp_merge(state, cover=()):
    (keep_a, send_a), (keep_b, send_b), near, far = state
    got_a = after(swap(send_a, "dp", near), *cover)
    got_b = after(swap(send_b, "dp", far), *cover)
    return merge(keep_a, got_a), merge(keep_b, got_b)


def row_partial(inputs, grads):
    row_n = lax.axis_size("row")
    if row_n != 2:
        whole = mat(inputs, grads, (0, 0), BF16)
        return whole, scatter_down(whole.reshape(row_n, -1, whole.shape[1]), "row")
    size = inputs.shape[1] // 2
    mine = lax.axis_index("row")
    theirs = lax.dynamic_slice_in_dim(inputs, (1 - mine) * size, size, 1)
    send = mat(theirs, grads, (0, 0), BF16)
    own = lax.dynamic_slice_in_dim(inputs, mine * size, size, 1)
    return send, (mat(own, after(grads, send), (0, 0)) + swap(send, "row", 1).astype(F32)).astype(BF16)


def fold(block, rows):
    return jnp.transpose(block.reshape(-1, rows, block.shape[1]), (1, 0, 2)).reshape(rows, -1)


def unfold(block, cols):
    rows = block.shape[0]
    return jnp.transpose(block.reshape(rows, -1, cols), (1, 0, 2)).reshape(-1, cols)


def lane_plan(widths, col_n):
    plan, wide_at, own_at = [], 0, 0
    for width, groups in widths:
        size = width // col_n
        for group in range(groups):
            for col in range(col_n):
                plan.append((wide_at + group * width + col * size, col, own_at, size))
            own_at += size
        wide_at += groups * width
    return plan, wide_at, own_at


def to_cols_kernel(in_ref, out_ref, *, plan):
    for wide, col, own, size in plan:
        out_ref[col, :, :, own : own + size] = in_ref[:, :, wide : wide + size]


def from_cols_kernel(in_ref, out_ref, *, plan):
    for wide, col, own, size in plan:
        out_ref[:, :, wide : wide + size] = in_ref[col, :, :, own : own + size]


def to_cols(pair, widths):
    col_n = lax.axis_size("col")
    plan, _, own = lane_plan(widths, col_n)
    return pl.pallas_call(
        partial(to_cols_kernel, plan=plan),
        name="to_cols",
        out_shape=jax.ShapeDtypeStruct((col_n,) + pair.shape[:2] + (own,), pair.dtype),
    )(pair)


def from_cols(wide, widths):
    plan, lanes, _ = lane_plan(widths, lax.axis_size("col"))
    return pl.pallas_call(
        partial(from_cols_kernel, plan=plan),
        name="from_cols",
        out_shape=jax.ShapeDtypeStruct(wide.shape[1:3] + (lanes,), wide.dtype),
    )(wide)


def fetch_vectors(parts):
    sizes = [p.shape[0] for p in parts]
    flat = gather_up(gather_down(jnp.concatenate(parts), "col"), "row")
    flat = flat.reshape(-1, flat.shape[-1])
    out, at = [], 0
    for size in sizes:
        out.append(flat[:, at : at + size].reshape(-1).astype(F32))
        at += size
    return out


def line_up(parts, rows):
    row_n, col_n = lax.axis_size("row"), lax.axis_size("col")
    flat = jnp.concatenate([p.reshape(row_n * col_n, -1) for p in parts], axis=1)
    flat = scatter_down(flat.reshape(row_n, col_n, -1).astype(BF16), "row")
    flat = jnp.transpose(flat.reshape(col_n, -1, 128 // col_n), (1, 0, 2)).reshape(-1, 128)
    return jnp.pad(flat, ((0, rows - flat.shape[0]), (0, 0)))


def take_apart(block, parts):
    blocks = lax.axis_size("row") * lax.axis_size("col")
    sizes = [p.shape[0] // blocks for p in parts]
    flat = block[: sum(sizes) // block.shape[1]].reshape(-1).astype(F32)
    out, at = [], 0
    for size in sizes:
        out.append(flat[at : at + size])
        at += size
    return out


CHUNK = 256
PARTS = ((0, 2), (2, 3), (5, 1))
KEPT = [pl.BlockSpec(memory_space=pl.ANY)]


def attend_kernel(q_ref, k_ref, v_ref, a_ref, b_ref, *refs, dim):
    o_ref, e_ref, inv_ref = refs[-3:]
    length = q_ref.shape[0]
    low_lane = lax.broadcasted_iota(jnp.int32, (length, 2 * dim), 1) < dim
    low_row = lax.broadcasted_iota(jnp.int32, (2 * dim, length), 0) < dim
    queries = q_ref[...].astype(F32) * (dim**-0.5)
    keys = k_ref[...].astype(F32)
    marks_q = a_ref[...].astype(F32)
    marks_k = b_ref[...].astype(F32)
    values_t = jnp.transpose(v_ref[...].astype(F32))
    inv_ref[...] = jnp.zeros(inv_ref.shape, F32)
    halves = []
    for head in range(2):
        lanes = low_lane if head == 0 else ~low_lane
        rows = low_row if head == 0 else ~low_row
        q_ext = jnp.where(lanes, queries, marks_q).astype(BF16)
        k_ext = jnp.where(lanes, keys, marks_k).astype(BF16)
        v_ext = jnp.where(rows, values_t, 1.0).astype(BF16)
        pieces = []
        for at in range(0, length, CHUNK):
            scores = mat(k_ext, q_ext[at : at + CHUNK], (1, 1))
            peak = jnp.maximum(jnp.max(scores, axis=0, keepdims=True), FLOOR)
            weights = jnp.exp(scores - peak).astype(BF16)
            e_ref[head, :, at : at + CHUNK] = weights
            out = mat(v_ext, weights, (1, 0))
            own = out[head * dim : (head + 1) * dim]
            total = out[dim : dim + 1] if head == 0 else out[0:1]
            live = total > 0.0
            inv = jnp.where(live, 1.0 / jnp.where(live, total, 1.0), 0.0)
            inv_ref[0, head : head + 1, at : at + CHUNK] = inv
            alone = values_t[head * dim : (head + 1) * dim, at : at + CHUNK]
            pieces.append(jnp.where(live, own * inv, alone))
        halves.append(jnp.concatenate(pieces, axis=1))
    o_ref[...] = jnp.transpose(jnp.concatenate(halves, axis=0)).astype(BF16)


def attend(mixed, marks_q, marks_k, first, part, so_far):
    count, width3 = mixed.shape
    width = width3 // 3
    seq_n = count // SEQ
    dim = width // HEADS
    pairs = HEADS // 2
    span = 2 * dim
    col = lambda shift: pl.BlockSpec((SEQ, span), lambda s, p: (s, p + first + shift))
    mark = pl.BlockSpec((SEQ, span), lambda s, p: (s, 0))
    return pl.pallas_call(
        partial(attend_kernel, dim=dim),
        name="attend",
        grid=(seq_n, part),
        in_specs=[col(0), col(pairs), col(2 * pairs), mark, mark] + KEPT * len(so_far),
        input_output_aliases={5 + i: i for i in range(len(so_far))},
        out_specs=[
            col(0),
            pl.BlockSpec((2, SEQ, SEQ), lambda s, p: (s * part + p, 0, 0)),
            pl.BlockSpec((1, 8, SEQ), lambda s, p: (s * part + p, 0, 0)),
        ],
        out_shape=[
            jax.ShapeDtypeStruct((count, width), BF16),
            jax.ShapeDtypeStruct((seq_n * part * 2, SEQ, SEQ), BF16),
            jax.ShapeDtypeStruct((seq_n * part, 8, SEQ), F32),
        ],
        cost_estimate=pl.CostEstimate(
            flops=7_000_000_000 * part, transcendentals=0, bytes_accessed=5_000_000 * part
        ),
    )(mixed, mixed, mixed, marks_q, marks_k, *so_far)


def attend_back_kernel(
    q_ref, k_ref, v_ref, o_ref, g_ref, a_ref, e_ref, inv_ref, *refs, dim
):
    dq_ref, dk_ref, dv_ref = refs[-3:]
    length = q_ref.shape[0]
    low_lane = lax.broadcasted_iota(jnp.int32, (length, 2 * dim), 1) < dim
    scale = dim**-0.5
    grads = g_ref[...].astype(F32)
    grads_t = jnp.transpose(grads)
    outs_t = jnp.transpose(o_ref[...].astype(F32))
    keys_t = jnp.transpose(k_ref[...].astype(F32)).astype(BF16)
    values = v_ref[...].astype(F32)
    queries = q_ref[...]
    inv = inv_ref[0]
    row_id = lax.broadcasted_iota(jnp.int32, (dim, length), 0)
    dq_halves, dk_halves, dv_halves = [], [], []
    for head in range(2):
        part = slice(head * dim, (head + 1) * dim)
        lanes = low_lane if head == 0 else ~low_lane
        grad_low = (grads_t[part] * inv[head : head + 1]).astype(BF16)
        inner = -jnp.sum(grad_low.astype(F32) * outs_t[part], axis=0, keepdims=True)
        high = inner.astype(BF16).astype(F32)
        rest = inner - high
        mid = rest.astype(BF16).astype(F32)
        last = rest - mid
        extra = jnp.where(
            row_id == 0, high, jnp.where(row_id == 1, mid, jnp.where(row_id == 2, last, 0.0))
        ).astype(BF16)
        right = jnp.concatenate([grad_low, extra] if head == 0 else [extra, grad_low], axis=0)
        v_ext = jnp.where(lanes, values, 1.0).astype(BF16)
        grad_pair = jnp.concatenate([grad_low, grad_low], axis=0)
        d_keys = jnp.zeros((length, 2 * dim), F32)
        d_values = jnp.zeros((length, 2 * dim), F32)
        dq_parts = []
        for at in range(0, length, CHUNK):
            weights = e_ref[head, :, at : at + CHUNK]
            d_probs = mat(v_ext, right[:, at : at + CHUNK], (1, 0))
            d_scores = weights * d_probs.astype(BF16)
            dq_parts.append(mat(keys_t[part], d_scores, (1, 0)))
            d_keys = d_keys + mat(d_scores, queries[at : at + CHUNK], (1, 0))
            d_values = d_values + mat(weights, grad_pair[:, at : at + CHUNK], (1, 1))
        dq_halves.append(jnp.concatenate(dq_parts, axis=1))
        dk_halves.append(d_keys)
        dv_halves.append(d_values)
    dq_ref[...] = (jnp.transpose(jnp.concatenate(dq_halves, axis=0)) * scale).astype(BF16)
    dk_ref[...] = (jnp.where(low_lane, dk_halves[0], dk_halves[1]) * scale).astype(BF16)
    alone = a_ref[:, 0:1].astype(F32) > 0.0
    d_values = jnp.where(low_lane, dv_halves[0], dv_halves[1])
    dv_ref[...] = jnp.where(alone, grads, d_values).astype(BF16)


def attend_back(mixed, outs, grads, marks_q, weights, inv, first, part, so_far):
    count, width3 = mixed.shape
    width = width3 // 3
    seq_n = count // SEQ
    dim = width // HEADS
    pairs = HEADS // 2
    span = 2 * dim
    col = lambda shift: pl.BlockSpec((SEQ, span), lambda s, p: (s, p + first + shift))
    return pl.pallas_call(
        partial(attend_back_kernel, dim=dim),
        name="attend_back",
        grid=(seq_n, part),
        in_specs=[
            col(0),
            col(pairs),
            col(2 * pairs),
            col(0),
            col(0),
            pl.BlockSpec((SEQ, span), lambda s, p: (s, 0)),
            pl.BlockSpec((2, SEQ, SEQ), lambda s, p: (s * part + p, 0, 0)),
            pl.BlockSpec((1, 8, SEQ), lambda s, p: (s * part + p, 0, 0)),
        ]
        + KEPT * len(so_far),
        input_output_aliases={8 + i: i for i in range(len(so_far))},
        out_specs=[col(0), col(0), col(0)],
        out_shape=[jax.ShapeDtypeStruct((count, width), BF16)] * 3,
        cost_estimate=pl.CostEstimate(
            flops=7_000_000_000 * part, transcendentals=0, bytes_accessed=6_000_000 * part
        ),
    )(mixed, mixed, mixed, outs, grads, marks_q, weights, inv, *so_far)


def up_kernel(x_ref, w_ref, b_ref, act_ref, slope_ref):
    pre = mat(x_ref[...], w_ref[...], (1, 0)) + b_ref[...]
    cdf = 0.5 * (1.0 + lax.erf(pre * (0.5**0.5)))
    act_ref[...] = (pre * cdf).astype(BF16)
    density = jnp.exp(pre * pre * -0.5) * 0.3989422804014327
    slope_ref[...] = (cdf + pre * density).astype(BF16)


def up_project(normed_low, up_weight, up_bias):
    count, width = normed_low.shape
    hidden = up_weight.shape[1]
    rows, tile = min(count, 1024), 256
    spec = pl.BlockSpec((rows, tile), lambda r, f: (r, f))
    return pl.pallas_call(
        up_kernel,
        name="up_project",
        grid=(count // rows, hidden // tile),
        in_specs=[
            pl.BlockSpec((rows, width), lambda r, f: (r, 0)),
            pl.BlockSpec((width, tile), lambda r, f: (0, f)),
            pl.BlockSpec((1, tile), lambda r, f: (0, f)),
        ],
        out_specs=[spec, spec],
        out_shape=[jax.ShapeDtypeStruct((count, hidden), BF16)] * 2,
        cost_estimate=pl.CostEstimate(
            flops=20_000_000_000, transcendentals=0, bytes_accessed=20_000_000
        ),
    )(normed_low, up_weight, up_bias[None])


def per_device(
    tokens,
    segments,
    cotangent,
    qkv_weight,
    out_weight,
    up_weight,
    down_weight,
    qv_bias,
    out_bias,
    norm1_gain,
    norm1_shift,
    up_bias,
    down_bias,
    norm2_gain,
    norm2_shift,
):
    count, width = tokens.shape
    rows, ff = up_weight.shape[0], down_weight.shape[0] // up_weight.shape[0]
    col_n = lax.axis_size("col")
    hidden = up_weight.shape[1] * col_n
    wide_ffn = [(hidden, 1), (width, ff), (width, 1)]
    vector_parts = [
        qv_bias,
        out_bias,
        norm1_gain,
        norm1_shift,
        up_bias,
        down_bias,
        norm2_gain,
        norm2_shift,
    ]
    dp_count = lax.axis_size("dp")
    down_piece = lax.dynamic_index_in_dim(
        down_weight.reshape(ff, 2, dp_count, rows // (2 * dp_count), -1),
        lax.axis_index("dp"),
        2,
        keepdims=False,
    )
    qkv_cols = own_piece(qkv_weight)[None]
    col_steps = steps_up("col")[::-1]
    for index, step in enumerate(col_steps):
        qkv_cols = widen(qkv_cols, "col", step, 1)
        qkv_cols = qkv_cols.reshape((-1,) + qkv_cols.shape[2:])
        if index == 0:
            qkv_cols, *vector_parts = tie(qkv_cols, *vector_parts)
    qkv_cols, up_piece, down_piece, out_piece = tie(
        qkv_cols, own_piece(up_weight), down_piece, own_piece(out_weight)
    )
    (qv_full, out_full, gain_one, shift_one, up_full, down_full, gain_two, shift_two) = (
        fetch_vectors(vector_parts)
    )
    qkv_full = join_rows(rows_of(gather_dp(from_cols(qkv_cols, [(3 * width, 1)]))))
    packed = jnp.concatenate([up_piece] + [d for d in down_piece] + [out_piece], axis=2)
    ffn_pair = from_cols(gather_down(packed, "col"), wide_ffn)

    lane = lax.broadcasted_iota(jnp.int32, (count, 128), 1) % 64
    seg = segments[:, None]
    marks_q = (seg == lane).astype(BF16)
    marks_k = jnp.where((seg == lane) & (lane != 0), 0.0, NEG).astype(BF16)

    tokens_low = tokens.astype(BF16)
    mix_bias = jnp.concatenate([qv_full[:width], jnp.zeros((width,), F32), qv_full[width:]])
    mixed = (mat(tokens_low, qkv_full, (1, 0)) + mix_bias).astype(BF16)
    dp_steps = len(steps_up("dp"))
    kept, ffn_now = [], (ffn_pair[0][None], ffn_pair[1][None])
    for index, (first, part) in enumerate(PARTS):
        so_far = (kept[-1][0],) if kept else ()
        kept.append(attend(after(mixed, ffn_now), marks_q, marks_k, first, part, so_far))
        if index < dp_steps:
            ffn_now = gather_dp_step(*ffn_now, index, (kept[-1][2],))
        if index == dp_steps - 1:
            ffn_half = rows_of(ffn_now)
            ffn_now = (
                ffn_half[:, :hidden],
                unfold(ffn_half[:, hidden : hidden + ff * width], width),
                ffn_half[:, hidden + ff * width :],
            )
    up_mat, down_mat, out_mat = (join_rows(m, (kept[-1][2],)) for m in ffn_now)
    attn_low = kept[-1][0]
    first_sum = tokens + mat(attn_low, out_mat, (1, 0)) + out_full
    normed, norm_one_pull = jax.vjp(layer_norm, first_sum, gain_one, shift_one)
    normed_low = normed.astype(BF16)
    act_low, slope = up_project(normed_low, up_mat, up_full)
    second_sum = normed + mat(act_low, down_mat, (1, 0)) + down_full
    layer_out, norm_two_pull = jax.vjp(layer_norm, second_sum, gain_two, shift_two)
    live_rows = (segments != 0).astype(F32)[:, None]
    d_second, d_gain_two, d_shift_two = norm_two_pull(cotangent * live_rows)
    d_feed = d_second.astype(BF16)

    dp_n = lax.axis_size("dp")
    down_send, down_half = row_partial(act_low, d_feed)
    grad_down_bias = jnp.sum(d_feed.astype(F32), axis=0)
    d_act = mat(d_feed, down_mat, (1, 1))
    d_pre_low = (d_act * slope.astype(F32)).astype(BF16)
    up_send, up_half = row_partial(normed_low, d_pre_low)
    grad_up_bias = jnp.sum(d_pre_low.astype(F32), axis=0)
    d_normed = d_second + mat(after(d_pre_low, down_send, up_send), up_mat, (1, 1))
    d_first, d_gain_one, d_shift_one = norm_one_pull(d_normed)
    d_branch = d_first.astype(BF16)
    grad_out_bias = jnp.sum(d_branch.astype(F32), axis=0)
    d_attended = mat(d_branch, out_mat, (1, 1)).astype(BF16)

    half = jnp.concatenate([up_half, fold(down_half, rows)], axis=1)
    half = half.reshape(2, dp_n, -1, half.shape[1])
    pair, results = (half[0], half[1]), [()]
    out_send, out_half = row_partial(attn_low, d_branch)

    def back_part(which, gate):
        first, part = PARTS[which]
        _, weights, inv = kept[which]
        grads = after(d_attended, gate)
        so_far = results[-1]
        results.append(
            attend_back(mixed, attn_low, grads, marks_q, weights, inv, first, part, so_far)
        )
        return tuple(results[-1][:1])

    for index in range(dp_steps):
        state = scatter_dp_sends(pair, index)
        pair = scatter_dp_merge(state, back_part((1, 0)[index], (state[:2], (out_send, out_half)[index])))
    ffn_cols = to_cols(jnp.stack([pair[0][0], pair[1][0]]), wide_ffn[:2])
    near = steps_up("col")[0]
    keep, send = split(ffn_cols.reshape((-1, 2) + ffn_cols.shape[1:]), "col", near, 1)
    ffn_cols = merge(keep, after(swap(send, "col", near), *back_part(2, send)))
    dq_low, dk_low, dv_low = results[-1]
    d_mixed = after(jnp.concatenate([dq_low, dk_low, dv_low], axis=1), ffn_cols)
    grad_qv_bias = jnp.concatenate(
        [jnp.sum(dq_low.astype(F32), axis=0), jnp.sum(dv_low.astype(F32), axis=0)]
    )
    vectors = [
        grad_qv_bias,
        grad_up_bias,
        grad_down_bias,
        d_gain_two,
        d_shift_two,
        grad_out_bias,
        d_gain_one,
        d_shift_one,
    ]
    _, qkv_half = row_partial(tokens_low, d_mixed)
    half = jnp.concatenate([qkv_half, out_half, line_up(vectors, rows)], axis=1)
    half = half.reshape(2, dp_n, -1, half.shape[1])
    pair = (half[0], half[1])
    ffn_waits = []
    for far in steps_up("col")[1:]:
        keep, send = split(ffn_cols.reshape((-1, 2) + ffn_cols.shape[1:]), "col", far, 1)
        ffn_waits.append((keep, swap(send, "col", far)))
        if far != steps_up("col")[-1]:
            ffn_cols = merge(*ffn_waits[-1])
    for index in range(dp_steps):
        (keep_a, send_a), (keep_b, send_b), near, far = scatter_dp_sends(pair, index)
        cover = ()
        if index == 0:
            send_a, send_b, late_mixed = tie(send_a, send_b, d_mixed)
            token_grad = d_first + mat(late_mixed, qkv_full, (1, 1))
            cover = (token_grad,)
        pair = scatter_dp_merge(((keep_a, send_a), (keep_b, send_b), near, far), cover)
        if index == 0 and ffn_waits:
            keep, got = ffn_waits[-1]
            got, *pair = tie(got, *pair)
            ffn_cols = merge(keep, got)
    attn_wide = [(3 * width, 1), (width, 1), (128, 1)]
    attn_cols = to_cols(jnp.stack([pair[0][0], pair[1][0]]), attn_wide)
    ffn_own, attn_cols = tie(ffn_cols[0], attn_cols)
    ffn_state = (ffn_own[0][None], ffn_own[1][None])
    for index, step in enumerate(steps_up("col")):
        keep, send = split(attn_cols.reshape((-1, 2) + attn_cols.shape[1:]), "col", step, 1)
        got = swap(send, "col", step)
        if index < dp_steps:
            ffn_state = gather_dp_step(*ffn_state, index, (got,))
        attn_cols = merge(keep, got)
    for index in range(len(steps_up("col")), dp_steps):
        ffn_state = gather_dp_step(*ffn_state, index)
    ffn_grad = rows_of(ffn_state)
    attn_grad = rows_of(gather_dp(attn_cols[0]))
    grad_up = ffn_grad[:, : hidden // col_n].astype(F32)
    grad_down = unfold(ffn_grad[:, hidden // col_n :], width // col_n).astype(F32)
    grad_qkv = attn_grad[:, : 3 * width // col_n].astype(F32)
    grad_out = attn_grad[:, 3 * width // col_n : 4 * width // col_n].astype(F32)
    (
        grad_qv_bias,
        grad_up_bias,
        grad_down_bias,
        d_gain_two,
        d_shift_two,
        grad_out_bias,
        d_gain_one,
        d_shift_one,
    ) = take_apart(attn_grad[:, 4 * width // col_n :], vectors)
    return (
        layer_out,
        token_grad,
        grad_qkv,
        grad_out,
        grad_up,
        grad_down,
        grad_qv_bias,
        grad_out_bias,
        d_gain_one,
        d_shift_one,
        grad_up_bias,
        grad_down_bias,
        d_gain_two,
        d_shift_two,
    )


def solution(mesh):
    tokens = P(("dp", "row", "col"), None)
    block = P("row", "col")
    vector = P(("row", "col"))
    return jax.shard_map(
        per_device,
        mesh=mesh,
        in_specs=(tokens, P(("dp", "row", "col")), tokens) + (block,) * 4 + (vector,) * 8,
        out_specs=(tokens, tokens) + (block,) * 4 + (vector,) * 8,
        check_vma=False,
    )
```

```python
from functools import partial

import jax
import jax.numpy as jnp
from jax import lax
from jax.experimental import pallas as pl
from jax.experimental.pallas import tpu as pltpu
from jax.sharding import PartitionSpec as P

HEADS = 12
SEQ = 1024
EPS = 1e-05
NEG = -1e30
FLOOR = -1e29

F32 = jnp.float32
BF16 = jnp.bfloat16


def layer_norm(hidden, gain, shift):
    center = hidden - jnp.mean(hidden, axis=-1, keepdims=True)
    spread = jnp.mean(center * center, axis=-1, keepdims=True)
    return center * lax.rsqrt(spread + EPS) * gain + shift


def mat(left, right, dims, kind=F32):
    return lax.dot_general(left, right, ((dims[:1], dims[1:]), ((), ())), preferred_element_type=kind)


def swap(value, axis, step):
    count = lax.axis_size(axis)
    return lax.ppermute(value, axis, [(i, i ^ step) for i in range(count)])


def steps_up(axis):
    count, out, step = lax.axis_size(axis), [], 1
    while step < count:
        out.append(step)
        step *= 2
    return out


def bit_of(axis, step):
    return (lax.axis_index(axis) // step) % 2


def after(value, *tokens):
    return lax.optimization_barrier((value, tokens))[0]


def tie(*values):
    return lax.optimization_barrier(values)


def widen(value, axis, step, at, cover=()):
    other = after(swap(value, axis, step), *cover)
    mine_low = bit_of(axis, step) == 0
    return jnp.where(mine_low, jnp.stack([value, other], at), jnp.stack([other, value], at))


def gather_up(value, axis):
    value = value[None]
    for step in steps_up(axis):
        value = widen(value, axis, step, 0)
        value = value.reshape((-1,) + value.shape[2:])
    return value


def gather_down(value, axis):
    value = value[None]
    for step in steps_up(axis)[::-1]:
        value = widen(value, axis, step, 1)
        value = value.reshape((-1,) + value.shape[2:])
    return value


def split(value, axis, step, at):
    bit = bit_of(axis, step)
    keep = lax.dynamic_index_in_dim(value, bit, at, keepdims=False)
    return keep, lax.dynamic_index_in_dim(value, 1 - bit, at, keepdims=False)


def merge(keep, got):
    return (keep.astype(F32) + got.astype(F32)).astype(keep.dtype)


def halve(value, axis, step, at):
    keep, send = split(value, axis, step, at)
    return merge(keep, swap(send, axis, step))


def scatter_up(value, axis):
    for step in steps_up(axis):
        value = value.reshape((value.shape[0] // 2, 2) + value.shape[1:])
        value = halve(value, axis, step, 1)
    return value[0]


def scatter_down(value, axis):
    for step in steps_up(axis)[::-1]:
        value = value.reshape((2, value.shape[0] // 2) + value.shape[1:])
        value = halve(value, axis, step, 0)
    return value[0]


def own_piece(block):
    rows, cols = block.shape
    dp_n = lax.axis_size("dp")
    return lax.dynamic_index_in_dim(
        block.reshape(2, dp_n, rows // (2 * dp_n), cols), lax.axis_index("dp"), 1, keepdims=False
    )


def gather_dp_step(first, second, index, cover=()):
    ups = steps_up("dp")
    first = widen(first, "dp", ups[-1 - index], 1, cover)
    second = widen(second, "dp", ups[index], 0, cover)
    return first.reshape((-1,) + first.shape[2:]), second.reshape((-1,) + second.shape[2:])


def gather_dp(pair):
    state = (pair[0][None], pair[1][None])
    for index in range(len(steps_up("dp"))):
        state = gather_dp_step(*state, index)
    return state


def rows_of(pair):
    return jnp.stack(pair).reshape(-1, pair[0].shape[-1])


def join_rows(half, cover=()):
    whole = half[None]
    for step in steps_up("row"):
        whole = widen(whole, "row", step, 0, cover)
        whole = whole.reshape((-1,) + whole.shape[2:])
    return whole.reshape(-1, whole.shape[-1])


def scatter_dp_sends(pair, index):
    first, second = pair
    ups = steps_up("dp")
    near, far = ups[index], ups[-1 - index]
    first = first.reshape((first.shape[0] // 2, 2) + first.shape[1:])
    second = second.reshape((2, second.shape[0] // 2) + second.shape[1:])
    return split(first, "dp", near, 1), split(second, "dp", far, 0), near, far


def scatter_dp_merge(state, cover=()):
    (keep_a, send_a), (keep_b, send_b), near, far = state
    got_a = after(swap(send_a, "dp", near), *cover)
    got_b = after(swap(send_b, "dp", far), *cover)
    return merge(keep_a, got_a), merge(keep_b, got_b)


def row_partial(inputs, grads):
    row_n = lax.axis_size("row")
    if row_n != 2:
        whole = mat(inputs, grads, (0, 0), BF16)
        return whole, scatter_down(whole.reshape(row_n, -1, whole.shape[1]), "row")
    size = inputs.shape[1] // 2
    mine = lax.axis_index("row")
    theirs = lax.dynamic_slice_in_dim(inputs, (1 - mine) * size, size, 1)
    send = mat(theirs, grads, (0, 0), BF16)
    own = lax.dynamic_slice_in_dim(inputs, mine * size, size, 1)
    return send, (mat(own, after(grads, send), (0, 0)) + swap(send, "row", 1).astype(F32)).astype(BF16)


def fold(block, rows):
    return jnp.transpose(block.reshape(-1, rows, block.shape[1]), (1, 0, 2)).reshape(rows, -1)


def unfold(block, cols):
    rows = block.shape[0]
    return jnp.transpose(block.reshape(rows, -1, cols), (1, 0, 2)).reshape(-1, cols)


def lane_plan(widths, col_n):
    plan, wide_at, own_at = [], 0, 0
    for width, groups in widths:
        size = width // col_n
        for group in range(groups):
            for col in range(col_n):
                plan.append((wide_at + group * width + col * size, col, own_at, size))
            own_at += size
        wide_at += groups * width
    return plan, wide_at, own_at


def to_cols_kernel(in_ref, out_ref, *, plan):
    for wide, col, own, size in plan:
        out_ref[col, :, :, own : own + size] = in_ref[:, :, wide : wide + size]


def from_cols_kernel(in_ref, out_ref, *, plan):
    for wide, col, own, size in plan:
        out_ref[:, :, wide : wide + size] = in_ref[col, :, :, own : own + size]


def to_cols(pair, widths):
    col_n = lax.axis_size("col")
    plan, _, own = lane_plan(widths, col_n)
    return pl.pallas_call(
        partial(to_cols_kernel, plan=plan),
        name="to_cols",
        out_shape=jax.ShapeDtypeStruct((col_n,) + pair.shape[:2] + (own,), pair.dtype),
    )(pair)


def from_cols(wide, widths):
    plan, lanes, _ = lane_plan(widths, lax.axis_size("col"))
    return pl.pallas_call(
        partial(from_cols_kernel, plan=plan),
        name="from_cols",
        out_shape=jax.ShapeDtypeStruct(wide.shape[1:3] + (lanes,), wide.dtype),
    )(wide)


def fetch_vectors(parts):
    sizes = [p.shape[0] for p in parts]
    flat = gather_up(gather_down(jnp.concatenate(parts), "col"), "row")
    flat = flat.reshape(-1, flat.shape[-1])
    out, at = [], 0
    for size in sizes:
        out.append(flat[:, at : at + size].reshape(-1).astype(F32))
        at += size
    return out


def line_up(parts, rows):
    row_n, col_n = lax.axis_size("row"), lax.axis_size("col")
    flat = jnp.concatenate([p.reshape(row_n * col_n, -1) for p in parts], axis=1)
    flat = scatter_down(flat.reshape(row_n, col_n, -1).astype(BF16), "row")
    flat = jnp.transpose(flat.reshape(col_n, -1, 128 // col_n), (1, 0, 2)).reshape(-1, 128)
    return jnp.pad(flat, ((0, rows - flat.shape[0]), (0, 0)))


def take_apart(block, parts):
    blocks = lax.axis_size("row") * lax.axis_size("col")
    sizes = [p.shape[0] // blocks for p in parts]
    flat = block[: sum(sizes) // block.shape[1]].reshape(-1).astype(F32)
    out, at = [], 0
    for size in sizes:
        out.append(flat[at : at + size])
        at += size
    return out


CHUNK = 1024
BACK_CHUNK = 512
PARTS = ((0, 2), (2, 3), (5, 1))
KEPT = [pl.BlockSpec(memory_space=pl.ANY)]


def attend_kernel(q_ref, k_ref, v_ref, a_ref, b_ref, *refs, dim):
    o_ref, e_ref, inv_ref = refs[-3:]
    length = q_ref.shape[0]
    low_lane = lax.broadcasted_iota(jnp.int32, (length, 2 * dim), 1) < dim
    low_row = lax.broadcasted_iota(jnp.int32, (2 * dim, length), 0) < dim
    queries = q_ref[...].astype(F32) * (dim**-0.5)
    keys = k_ref[...].astype(F32)
    marks_q = a_ref[...].astype(F32)
    marks_k = b_ref[...].astype(F32)
    values_t = jnp.transpose(v_ref[...].astype(F32))
    inv_ref[...] = jnp.zeros(inv_ref.shape, F32)
    halves = []
    for head in range(2):
        lanes = low_lane if head == 0 else ~low_lane
        rows = low_row if head == 0 else ~low_row
        q_ext = jnp.where(lanes, queries, marks_q).astype(BF16)
        k_ext = jnp.where(lanes, keys, marks_k).astype(BF16)
        v_ext = jnp.where(rows, values_t, 1.0).astype(BF16)
        pieces = []
        for at in range(0, length, CHUNK):
            scores = mat(k_ext, q_ext[at : at + CHUNK], (1, 1))
            peak = jnp.maximum(jnp.max(scores, axis=0, keepdims=True), FLOOR)
            weights = jnp.exp(scores - peak).astype(BF16)
            e_ref[head, :, at : at + CHUNK] = weights
            out = mat(v_ext, weights, (1, 0))
            own = out[head * dim : (head + 1) * dim]
            total = out[dim : dim + 1] if head == 0 else out[0:1]
            live = total > 0.0
            inv = jnp.where(live, 1.0 / jnp.where(live, total, 1.0), 0.0)
            inv_ref[0, head : head + 1, at : at + CHUNK] = inv
            alone = values_t[head * dim : (head + 1) * dim, at : at + CHUNK]
            pieces.append(jnp.where(live, own * inv, alone))
        halves.append(jnp.concatenate(pieces, axis=1))
    o_ref[...] = jnp.transpose(jnp.concatenate(halves, axis=0)).astype(BF16)


def attend(mixed, marks_q, marks_k, first, part, so_far):
    count, width3 = mixed.shape
    width = width3 // 3
    seq_n = count // SEQ
    dim = width // HEADS
    pairs = HEADS // 2
    span = 2 * dim
    col = lambda shift: pl.BlockSpec((SEQ, span), lambda s, p: (s, p + first + shift))
    mark = pl.BlockSpec((SEQ, span), lambda s, p: (s, 0))
    return pl.pallas_call(
        partial(attend_kernel, dim=dim),
        name="attend",
        grid=(seq_n, part),
        in_specs=[col(0), col(pairs), col(2 * pairs), mark, mark] + KEPT * len(so_far),
        input_output_aliases={5 + i: i for i in range(len(so_far))},
        out_specs=[
            col(0),
            pl.BlockSpec((2, SEQ, SEQ), lambda s, p: (s * part + p, 0, 0)),
            pl.BlockSpec((1, 8, SEQ), lambda s, p: (s * part + p, 0, 0)),
        ],
        out_shape=[
            jax.ShapeDtypeStruct((count, width), BF16),
            jax.ShapeDtypeStruct((seq_n * part * 2, SEQ, SEQ), BF16),
            jax.ShapeDtypeStruct((seq_n * part, 8, SEQ), F32),
        ],
        cost_estimate=pl.CostEstimate(
            flops=7_000_000_000 * part, transcendentals=0, bytes_accessed=5_000_000 * part
        ),
    )(mixed, mixed, mixed, marks_q, marks_k, *so_far)


def attend_back_kernel(
    q_ref, k_ref, v_ref, o_ref, g_ref, a_ref, e_ref, inv_ref, *refs, dim
):
    dq_ref, dk_ref, dv_ref = refs[-3:]
    length = q_ref.shape[0]
    low_lane = lax.broadcasted_iota(jnp.int32, (length, 2 * dim), 1) < dim
    scale = dim**-0.5
    grads = g_ref[...].astype(F32)
    grads_t = jnp.transpose(grads)
    outs_t = jnp.transpose(o_ref[...].astype(F32))
    keys_t = jnp.transpose(k_ref[...].astype(F32)).astype(BF16)
    values = v_ref[...].astype(F32)
    queries = q_ref[...]
    inv = inv_ref[0]
    row_id = lax.broadcasted_iota(jnp.int32, (dim, length), 0)
    dq_halves, dk_halves, dv_halves = [], [], []
    for head in range(2):
        part = slice(head * dim, (head + 1) * dim)
        lanes = low_lane if head == 0 else ~low_lane
        grad_low = (grads_t[part] * inv[head : head + 1]).astype(BF16)
        inner = -jnp.sum(grad_low.astype(F32) * outs_t[part], axis=0, keepdims=True)
        high = inner.astype(BF16).astype(F32)
        rest = inner - high
        mid = rest.astype(BF16).astype(F32)
        last = rest - mid
        extra = jnp.where(
            row_id == 0, high, jnp.where(row_id == 1, mid, jnp.where(row_id == 2, last, 0.0))
        ).astype(BF16)
        right = jnp.concatenate([grad_low, extra] if head == 0 else [extra, grad_low], axis=0)
        v_ext = jnp.where(lanes, values, 1.0).astype(BF16)
        grad_pair = jnp.concatenate([grad_low, grad_low], axis=0)
        d_keys = jnp.zeros((length, 2 * dim), F32)
        d_values = jnp.zeros((length, 2 * dim), F32)
        dq_parts = []
        for at in range(0, length, BACK_CHUNK):
            weights = e_ref[head, :, at : at + BACK_CHUNK]
            d_probs = mat(v_ext, right[:, at : at + BACK_CHUNK], (1, 0))
            d_scores = weights * d_probs.astype(BF16)
            dq_parts.append(mat(keys_t[part], d_scores, (1, 0)))
            d_keys = d_keys + mat(d_scores, queries[at : at + BACK_CHUNK], (1, 0))
            d_values = d_values + mat(weights, grad_pair[:, at : at + BACK_CHUNK], (1, 1))
        dq_halves.append(jnp.concatenate(dq_parts, axis=1))
        dk_halves.append(d_keys)
        dv_halves.append(d_values)
    dq_ref[...] = (jnp.transpose(jnp.concatenate(dq_halves, axis=0)) * scale).astype(BF16)
    dk_ref[...] = (jnp.where(low_lane, dk_halves[0], dk_halves[1]) * scale).astype(BF16)
    alone = a_ref[:, 0:1].astype(F32) > 0.0
    d_values = jnp.where(low_lane, dv_halves[0], dv_halves[1])
    dv_ref[...] = jnp.where(alone, grads, d_values).astype(BF16)


def attend_back(mixed, outs, grads, marks_q, weights, inv, first, part, so_far):
    count, width3 = mixed.shape
    width = width3 // 3
    seq_n = count // SEQ
    dim = width // HEADS
    pairs = HEADS // 2
    span = 2 * dim
    col = lambda shift: pl.BlockSpec((SEQ, span), lambda s, p: (s, p + first + shift))
    return pl.pallas_call(
        partial(attend_back_kernel, dim=dim),
        name="attend_back",
        grid=(seq_n, part),
        in_specs=[
            col(0),
            col(pairs),
            col(2 * pairs),
            col(0),
            col(0),
            pl.BlockSpec((SEQ, span), lambda s, p: (s, 0)),
            pl.BlockSpec((2, SEQ, SEQ), lambda s, p: (s * part + p, 0, 0)),
            pl.BlockSpec((1, 8, SEQ), lambda s, p: (s * part + p, 0, 0)),
        ]
        + KEPT * len(so_far),
        input_output_aliases={8 + i: i for i in range(len(so_far))},
        out_specs=[col(0), col(0), col(0)],
        out_shape=[jax.ShapeDtypeStruct((count, width), BF16)] * 3,
        cost_estimate=pl.CostEstimate(
            flops=7_000_000_000 * part, transcendentals=0, bytes_accessed=6_000_000 * part
        ),
    )(mixed, mixed, mixed, outs, grads, marks_q, weights, inv, *so_far)


def up_kernel(x_ref, w_ref, b_ref, act_ref, slope_ref):
    pre = mat(x_ref[...], w_ref[...], (1, 0)) + b_ref[...]
    cdf = 0.5 * (1.0 + lax.erf(pre * (0.5**0.5)))
    act_ref[...] = (pre * cdf).astype(BF16)
    density = jnp.exp(pre * pre * -0.5) * 0.3989422804014327
    slope_ref[...] = (cdf + pre * density).astype(BF16)


def up_project(normed_low, up_weight, up_bias):
    count, width = normed_low.shape
    hidden = up_weight.shape[1]
    rows, tile = min(count, 1024), 256
    spec = pl.BlockSpec((rows, tile), lambda r, f: (r, f))
    return pl.pallas_call(
        up_kernel,
        name="up_project",
        grid=(count // rows, hidden // tile),
        in_specs=[
            pl.BlockSpec((rows, width), lambda r, f: (r, 0)),
            pl.BlockSpec((width, tile), lambda r, f: (0, f)),
            pl.BlockSpec((1, tile), lambda r, f: (0, f)),
        ],
        out_specs=[spec, spec],
        out_shape=[jax.ShapeDtypeStruct((count, hidden), BF16)] * 2,
        cost_estimate=pl.CostEstimate(
            flops=20_000_000_000, transcendentals=0, bytes_accessed=20_000_000
        ),
    )(normed_low, up_weight, up_bias[None])


def per_device(
    tokens,
    segments,
    cotangent,
    qkv_weight,
    out_weight,
    up_weight,
    down_weight,
    qv_bias,
    out_bias,
    norm1_gain,
    norm1_shift,
    up_bias,
    down_bias,
    norm2_gain,
    norm2_shift,
):
    count, width = tokens.shape
    rows, ff = up_weight.shape[0], down_weight.shape[0] // up_weight.shape[0]
    col_n = lax.axis_size("col")
    hidden = up_weight.shape[1] * col_n
    wide_ffn = [(hidden, 1), (width, ff), (width, 1)]
    vector_parts = [
        qv_bias,
        out_bias,
        norm1_gain,
        norm1_shift,
        up_bias,
        down_bias,
        norm2_gain,
        norm2_shift,
    ]
    dp_count = lax.axis_size("dp")
    down_piece = lax.dynamic_index_in_dim(
        down_weight.reshape(ff, 2, dp_count, rows // (2 * dp_count), -1),
        lax.axis_index("dp"),
        2,
        keepdims=False,
    )
    qkv_cols = own_piece(qkv_weight)[None]
    col_steps = steps_up("col")[::-1]
    for index, step in enumerate(col_steps):
        qkv_cols = widen(qkv_cols, "col", step, 1)
        qkv_cols = qkv_cols.reshape((-1,) + qkv_cols.shape[2:])
        if index == 0:
            qkv_cols, *vector_parts = tie(qkv_cols, *vector_parts)
    qkv_cols, up_piece, down_piece, out_piece = tie(
        qkv_cols, own_piece(up_weight), down_piece, own_piece(out_weight)
    )
    (qv_full, out_full, gain_one, shift_one, up_full, down_full, gain_two, shift_two) = (
        fetch_vectors(vector_parts)
    )
    qkv_full = join_rows(rows_of(gather_dp(from_cols(qkv_cols, [(3 * width, 1)]))))
    packed = jnp.concatenate([up_piece] + [d for d in down_piece] + [out_piece], axis=2)
    ffn_pair = from_cols(gather_down(packed, "col"), wide_ffn)

    lane = lax.broadcasted_iota(jnp.int32, (count, 128), 1) % 64
    seg = segments[:, None]
    marks_q = (seg == lane).astype(BF16)
    marks_k = jnp.where((seg == lane) & (lane != 0), 0.0, NEG).astype(BF16)

    tokens_low = tokens.astype(BF16)
    mix_bias = jnp.concatenate([qv_full[:width], jnp.zeros((width,), F32), qv_full[width:]])
    mixed = (mat(tokens_low, qkv_full, (1, 0)) + mix_bias).astype(BF16)
    dp_steps = len(steps_up("dp"))
    kept, ffn_now = [], (ffn_pair[0][None], ffn_pair[1][None])
    for index, (first, part) in enumerate(PARTS):
        so_far = (kept[-1][0],) if kept else ()
        kept.append(attend(after(mixed, ffn_now), marks_q, marks_k, first, part, so_far))
        if index < dp_steps:
            ffn_now = gather_dp_step(*ffn_now, index, (kept[-1][2],))
        if index == dp_steps - 1:
            ffn_half = rows_of(ffn_now)
            ffn_now = (
                ffn_half[:, :hidden],
                unfold(ffn_half[:, hidden : hidden + ff * width], width),
                ffn_half[:, hidden + ff * width :],
            )
    up_mat, down_mat, out_mat = (join_rows(m, (kept[-1][2],)) for m in ffn_now)
    attn_low = kept[-1][0]
    first_sum = tokens + mat(attn_low, out_mat, (1, 0)) + out_full
    normed, norm_one_pull = jax.vjp(layer_norm, first_sum, gain_one, shift_one)
    normed_low = normed.astype(BF16)
    act_low, slope = up_project(normed_low, up_mat, up_full)
    second_sum = normed + mat(act_low, down_mat, (1, 0)) + down_full
    layer_out, norm_two_pull = jax.vjp(layer_norm, second_sum, gain_two, shift_two)
    live_rows = (segments != 0).astype(F32)[:, None]
    d_second, d_gain_two, d_shift_two = norm_two_pull(cotangent * live_rows)
    d_feed = d_second.astype(BF16)

    dp_n = lax.axis_size("dp")
    down_send, down_half = row_partial(act_low, d_feed)
    grad_down_bias = jnp.sum(d_feed.astype(F32), axis=0)
    d_act = mat(d_feed, down_mat, (1, 1))
    d_pre_low = (d_act * slope.astype(F32)).astype(BF16)
    up_send, up_half = row_partial(normed_low, d_pre_low)
    grad_up_bias = jnp.sum(d_pre_low.astype(F32), axis=0)
    d_normed = d_second + mat(after(d_pre_low, down_send, up_send), up_mat, (1, 1))
    d_first, d_gain_one, d_shift_one = norm_one_pull(d_normed)
    d_branch = d_first.astype(BF16)
    grad_out_bias = jnp.sum(d_branch.astype(F32), axis=0)
    d_attended = mat(d_branch, out_mat, (1, 1)).astype(BF16)

    half = jnp.concatenate([up_half, fold(down_half, rows)], axis=1)
    half = half.reshape(2, dp_n, -1, half.shape[1])
    pair, results = (half[0], half[1]), [()]
    out_send, out_half = row_partial(attn_low, d_branch)

    def back_part(which, gate):
        first, part = PARTS[which]
        _, weights, inv = kept[which]
        grads = after(d_attended, gate)
        so_far = results[-1]
        results.append(
            attend_back(mixed, attn_low, grads, marks_q, weights, inv, first, part, so_far)
        )
        return tuple(results[-1][:1])

    for index in range(dp_steps):
        state = scatter_dp_sends(pair, index)
        pair = scatter_dp_merge(state, back_part((1, 0)[index], (state[:2], (out_send, out_half)[index])))
    ffn_cols = to_cols(jnp.stack([pair[0][0], pair[1][0]]), wide_ffn[:2])
    near = steps_up("col")[0]
    keep, send = split(ffn_cols.reshape((-1, 2) + ffn_cols.shape[1:]), "col", near, 1)
    ffn_cols = merge(keep, after(swap(send, "col", near), *back_part(2, send)))
    dq_low, dk_low, dv_low = results[-1]
    d_mixed = after(jnp.concatenate([dq_low, dk_low, dv_low], axis=1), ffn_cols)
    grad_qv_bias = jnp.concatenate(
        [jnp.sum(dq_low.astype(F32), axis=0), jnp.sum(dv_low.astype(F32), axis=0)]
    )
    vectors = [
        grad_qv_bias,
        grad_up_bias,
        grad_down_bias,
        d_gain_two,
        d_shift_two,
        grad_out_bias,
        d_gain_one,
        d_shift_one,
    ]
    _, qkv_half = row_partial(tokens_low, d_mixed)
    half = jnp.concatenate([qkv_half, out_half, line_up(vectors, rows)], axis=1)
    half = half.reshape(2, dp_n, -1, half.shape[1])
    pair = (half[0], half[1])
    ffn_waits = []
    for far in steps_up("col")[1:]:
        keep, send = split(ffn_cols.reshape((-1, 2) + ffn_cols.shape[1:]), "col", far, 1)
        ffn_waits.append((keep, swap(send, "col", far)))
        if far != steps_up("col")[-1]:
            ffn_cols = merge(*ffn_waits[-1])
    for index in range(dp_steps):
        (keep_a, send_a), (keep_b, send_b), near, far = scatter_dp_sends(pair, index)
        cover = ()
        if index == 0:
            send_a, send_b, late_mixed = tie(send_a, send_b, d_mixed)
            token_grad = d_first + mat(late_mixed, qkv_full, (1, 1))
            cover = (token_grad,)
        pair = scatter_dp_merge(((keep_a, send_a), (keep_b, send_b), near, far), cover)
        if index == 0 and ffn_waits:
            keep, got = ffn_waits[-1]
            got, *pair = tie(got, *pair)
            ffn_cols = merge(keep, got)
    attn_wide = [(3 * width, 1), (width, 1), (128, 1)]
    attn_cols = to_cols(jnp.stack([pair[0][0], pair[1][0]]), attn_wide)
    ffn_own, attn_cols = tie(ffn_cols[0], attn_cols)
    ffn_state = (ffn_own[0][None], ffn_own[1][None])
    for index, step in enumerate(steps_up("col")):
        keep, send = split(attn_cols.reshape((-1, 2) + attn_cols.shape[1:]), "col", step, 1)
        got = swap(send, "col", step)
        if index < dp_steps:
            ffn_state = gather_dp_step(*ffn_state, index, (got,))
        attn_cols = merge(keep, got)
    for index in range(len(steps_up("col")), dp_steps):
        ffn_state = gather_dp_step(*ffn_state, index)
    ffn_grad = rows_of(ffn_state)
    attn_grad = rows_of(gather_dp(attn_cols[0]))
    grad_up = ffn_grad[:, : hidden // col_n].astype(F32)
    grad_down = unfold(ffn_grad[:, hidden // col_n :], width // col_n).astype(F32)
    grad_qkv = attn_grad[:, : 3 * width // col_n].astype(F32)
    grad_out = attn_grad[:, 3 * width // col_n : 4 * width // col_n].astype(F32)
    (
        grad_qv_bias,
        grad_up_bias,
        grad_down_bias,
        d_gain_two,
        d_shift_two,
        grad_out_bias,
        d_gain_one,
        d_shift_one,
    ) = take_apart(attn_grad[:, 4 * width // col_n :], vectors)
    return (
        layer_out,
        token_grad,
        grad_qkv,
        grad_out,
        grad_up,
        grad_down,
        grad_qv_bias,
        grad_out_bias,
        d_gain_one,
        d_shift_one,
        grad_up_bias,
        grad_down_bias,
        d_gain_two,
        d_shift_two,
    )


def solution(mesh):
    tokens = P(("dp", "row", "col"), None)
    block = P("row", "col")
    vector = P(("row", "col"))
    return jax.shard_map(
        per_device,
        mesh=mesh,
        in_specs=(tokens, P(("dp", "row", "col")), tokens) + (block,) * 4 + (vector,) * 8,
        out_specs=(tokens, tokens) + (block,) * 4 + (vector,) * 8,
        check_vma=False,
    )
```
